512 devices in a mesh: dp: 32 (over z, y_lo), seq: 16 (over x, y_hi, core).
Axes of the slice: x: 4, y: 4 (y_hi: 2, y_lo: 2; y = y_hi * 2 + y_lo), z: 16, core: 2. Of those that a mesh axis runs over, the one named last changes fastest.
Arguments:
- inputs: bfloat16 [64, 8192, 768], P('dp', 'seq'), may hold values from -6 to 6
- conv_weight: bfloat16 [3, 768, 384], P(None, 'dp', 'seq'), may hold values from -0.125 to 0.125
- point_weight: bfloat16 [384, 768], P('seq', 'dp'), may hold values from -0.3125 to 0.3125
- cotangent: bfloat16 [64, 8192, 768], P('dp', 'seq'), may hold values from -6 to 6
Outputs:
- input_grad: bfloat16 [64, 8192, 768], P('dp', 'seq')
- conv_grad: float32 [3, 768, 384], P(None, 'dp', 'seq')
The draws below stay inside these ranges and needn't reach their ends.
All inputs are finite; a program needn't handle non-finite values.
Results may differ from the reference program's by a relative error of at most 0.0054.
Values may be sent and summed in bfloat16 or wider, within the bound.
No kernel may reach another device: no remote copies, remote signals or barrier semaphores. Data moves between devices by JAX's collectives and lax.ppermute only.
A program may use at most 64 MiB of HBM per device.

```python
import jax
import jax.numpy as jnp
from jax import lax

C = 768
F = 384
SAMP_DEV = 2
DILATION = 1024
SAMPLES = 64
LENGTH = 8192
N_DP = 32


def block_levels(key, dims, split, low, top_value):
    loudness = 1.0
    for position, parts in split:
        draws = jax.random.uniform(jax.random.fold_in(jax.random.fold_in(key, 6), position), (parts,), jnp.float32, low / len(split), top_value / len(split))
        loudness = loudness * jnp.repeat(jnp.exp(draws), dims[position] // parts).reshape((-1,) + (1,) * (len(dims) - 1 - position))
    return loudness


def noise(stream_key, extent, deviation, bound, pieces=(), kind=jnp.bfloat16):
    drawn = deviation * jax.random.normal(stream_key, extent, jnp.float32)
    if pieces:
        drawn = drawn * block_levels(stream_key, extent, pieces, -0.22, 0.18)
    return jnp.clip(drawn, -bound, bound).astype(kind)


def setup_inputs(seed: int = 0) -> dict:
    arg_keys = jax.random.split(jax.random.key(seed), 5)
    inputs = noise(arg_keys[0], (SAMPLES, LENGTH, C), 1.0, 6.0, ((0, 32), (1, 16)))
    conv_weight = noise(arg_keys[1], (3, C, F), (3 * C) ** -0.5, 0.125, ((1, 32), (2, 16)))
    point_weight = noise(arg_keys[2], (F, C), F ** -0.5, 0.3125, ((0, 16), (1, 32)))
    cotangent = noise(arg_keys[3], (SAMPLES, LENGTH, C), 1.0, 6.0, ((0, 32), (1, 16)))
    return dict(inputs=inputs, conv_weight=conv_weight, point_weight=point_weight, cotangent=cotangent)


EPSILON = 1e-06
GELU_SCALE = 0.7978845608028654
GELU_CUBIC = 0.044715

def gelu_tanh(values):
    return 0.5 * values * (1.0 + jnp.tanh(GELU_SCALE * (values + GELU_CUBIC * values * values * values)))

def gelu_slope(values):
    tangent = jnp.tanh(GELU_SCALE * (values + GELU_CUBIC * values * values * values))
    return 0.5 * (1.0 + tangent) + 0.5 * values * (1.0 - tangent * tangent) * GELU_SCALE * (1.0 + 3.0 * GELU_CUBIC * values * values)

def from_lower(array, distance):
    return jnp.concatenate([jnp.zeros_like(array[:, :distance]), array[:, :-distance]], axis=1)

def from_upper(array, distance):
    return jnp.concatenate([array[:, distance:], jnp.zeros_like(array[:, :distance])], axis=1)

def product(left, right):
    return jnp.dot(left, right, preferred_element_type=jnp.float32)

def outer_sum(left, right):
    return jnp.dot(left.astype(jnp.float32).T, right.astype(jnp.float32))

def reference(inputs, conv_weight, point_weight, cotangent):
    grad_scale = float(SAMPLES * LENGTH) ** (-0.5)
    row_count = SAMP_DEV * LENGTH

    def one_group(conv_sum, group):
        group_inputs, group_cot = group
        floats = group_inputs.astype(jnp.float32)
        row_scale = lax.rsqrt(lax.optimization_barrier(jnp.mean(floats * floats, axis=-1, keepdims=True)) + EPSILON)
        normed = floats * row_scale
        acted = gelu_tanh(normed).astype(jnp.bfloat16)
        acted_flat = acted.reshape(row_count, C)
        tap_low = product(acted_flat, conv_weight[0]).astype(jnp.bfloat16).reshape(SAMP_DEV, LENGTH, F)
        tap_high = product(acted_flat, conv_weight[2]).astype(jnp.bfloat16).reshape(SAMP_DEV, LENGTH, F)
        shifted_low = from_lower(tap_low, DILATION).reshape(row_count, F).astype(jnp.float32)
        shifted_high = from_upper(tap_high, DILATION).reshape(row_count, F).astype(jnp.float32)
        preact = shifted_low + product(acted_flat, conv_weight[1]) + shifted_high
        cot_flat = group_cot.reshape(row_count, C)
        grad_inner = product(cot_flat, point_weight.T)
        grad_pre = (grad_inner * gelu_slope(preact)).astype(jnp.bfloat16)
        grad_blocks = grad_pre.reshape(SAMP_DEV, LENGTH, F)
        grad_upper = from_upper(grad_blocks, DILATION).reshape(row_count, F)
        grad_lower = from_lower(grad_blocks, DILATION).reshape(row_count, F)
        grad_act = product(grad_upper, conv_weight[0].T) + product(grad_pre, conv_weight[1].T) + product(grad_lower, conv_weight[2].T)
        normed_flat = normed.reshape(row_count, C)
        scale_flat = row_scale.reshape(row_count, 1)
        grad_norm = grad_act * gelu_slope(normed_flat)
        center = lax.optimization_barrier(jnp.mean(grad_norm * normed_flat, axis=-1, keepdims=True))
        grad_input = cot_flat.astype(jnp.float32) + scale_flat * (grad_norm - normed_flat * center)
        conv_terms = jnp.stack([outer_sum(acted_flat, grad_upper), outer_sum(acted_flat, grad_pre), outer_sum(acted_flat, grad_lower)], axis=0) * grad_scale
        return (conv_sum + conv_terms, grad_input.astype(jnp.bfloat16).reshape(SAMP_DEV, LENGTH, C))
    groups = (inputs.reshape(N_DP, SAMP_DEV, LENGTH, C), cotangent.reshape(N_DP, SAMP_DEV, LENGTH, C))
    conv_grad, grad_groups = lax.scan(one_group, jnp.zeros((3, C, F), jnp.float32), groups)
    return (grad_groups.reshape(SAMPLES, LENGTH, C), conv_grad)
```

```python
import jax
import jax.numpy as jnp
from jax import lax
from jax.sharding import PartitionSpec as P

SPAN = 2
LANES = 128

EPSILON = 1e-06
GELU_SCALE = 0.7978845608028654
GELU_CUBIC = 0.044715


def from_behind(x, axis, by):
    peers = lax.axis_size(axis)
    pairs = [(i, i + by) for i in range(peers) if 0 <= i + by < peers]
    return lax.ppermute(x, axis, pairs)


def gelu_tanh(values):
    return (
        0.5
        * values
        * (1.0 + jnp.tanh(GELU_SCALE * (values + GELU_CUBIC * values * values * values)))
    )


def gelu_slope(values):
    tangent = jnp.tanh(GELU_SCALE * (values + GELU_CUBIC * values * values * values))
    return 0.5 * (1.0 + tangent) + 0.5 * values * (1.0 - tangent * tangent) * GELU_SCALE * (
        1.0 + 3.0 * GELU_CUBIC * values * values
    )


def product(left, right):
    return lax.dot_general(left, right, (((1,), (0,)), ((), ())), preferred_element_type=jnp.float32)


def product_nt(left, right):
    return lax.dot_general(left, right, (((1,), (1,)), ((), ())), preferred_element_type=jnp.float32)


def product_tn(left, right):
    return lax.dot_general(left, right, (((0,), (0,)), ((), ())), preferred_element_type=jnp.float32)


def to_half(values):
    return lax.optimization_barrier(values.astype(jnp.bfloat16))


def everywhere(shard, axis):
    peers = lax.axis_size(axis)
    copies = jnp.broadcast_to(shard[None], (peers,) + shard.shape)
    return lax.all_to_all(copies, axis, 0, 0)


def normalize(inputs):
    floats = inputs.astype(jnp.float32)
    row_scale = lax.rsqrt(jnp.mean(floats * floats, axis=-1, keepdims=True) + EPSILON)
    return floats * row_scale, row_scale


def body(inputs, conv_weight, point_weight, cotangent):
    samp_count, bin_count, width = inputs.shape
    row_count = samp_count * bin_count
    n_dp, n_seq = lax.axis_size("dp"), lax.axis_size("seq")
    grad_scale = float(row_count * n_dp * n_seq) ** (-0.5)
    taps, c_part, f_part = conv_weight.shape
    hidden = f_part * n_seq

    tap_lanes = (taps + 1) * f_part
    shard = jnp.concatenate(
        [conv_weight[tap] for tap in range(taps)] + [point_weight.T], axis=1
    )
    shard = jnp.pad(shard, ((0, 0), (0, LANES - tap_lanes)))
    by_channel = everywhere(shard, "dp").reshape(width, LANES)
    by_tap = by_channel.T[:tap_lanes]
    gathered = everywhere(by_tap, "seq").reshape(n_seq, taps + 1, f_part, width)
    weights = jnp.transpose(gathered, (1, 0, 2, 3)).reshape(taps + 1, hidden, width)

    lower_in = from_behind(inputs, "seq", SPAN)
    upper_in = from_behind(inputs, "seq", -SPAN)

    normed, row_scale = normalize(inputs)
    acted = gelu_tanh(normed).astype(jnp.bfloat16).reshape(row_count, width)
    lower_acts = gelu_tanh(normalize(lower_in)[0]).astype(jnp.bfloat16).reshape(row_count, width)
    upper_acts = gelu_tanh(normalize(upper_in)[0]).astype(jnp.bfloat16).reshape(row_count, width)
    cot_flat = cotangent.reshape(row_count, width)

    grad_inner = product_nt(cot_flat, weights[3])
    shifted_low = to_half(product_nt(lower_acts, weights[0])).astype(jnp.float32)
    shifted_high = to_half(product_nt(upper_acts, weights[2])).astype(jnp.float32)
    preact = shifted_low + product_nt(acted, weights[1]) + shifted_high
    grad_pre = (grad_inner * gelu_slope(preact)).astype(jnp.bfloat16)

    terms = [
        (product_tn(grad_pre, acts) * grad_scale).astype(jnp.bfloat16)
        for acts in (lower_acts, acted, upper_acts)
    ]
    sums = [
        jnp.sum(
            lax.all_to_all(term.reshape(n_seq, f_part, width), "seq", 0, 0).astype(jnp.float32),
            axis=0,
        )
        for term in terms
    ]
    by_lane = jnp.concatenate(sums, axis=0).T
    by_lane = jnp.pad(by_lane, ((0, 0), (0, LANES - taps * f_part))).astype(jnp.bfloat16)
    parts = lax.all_to_all(by_lane.reshape(n_dp, c_part, LANES), "dp", 0, 0)
    total = jnp.sum(parts.astype(jnp.float32), axis=0)
    conv_grad = jnp.stack([total[:, t * f_part : (t + 1) * f_part] for t in range(taps)], axis=0)

    grad_blocks = grad_pre.reshape(samp_count, bin_count, hidden)
    grad_upper = from_behind(grad_blocks, "seq", -SPAN).reshape(row_count, hidden)
    grad_lower = from_behind(grad_blocks, "seq", SPAN).reshape(row_count, hidden)
    grad_act = (
        product(grad_upper, weights[0])
        + product(grad_pre, weights[1])
        + product(grad_lower, weights[2])
    )
    normed_flat = normed.reshape(row_count, width)
    scale_flat = row_scale.reshape(row_count, 1)
    grad_norm = grad_act * gelu_slope(normed_flat)
    center = jnp.mean(grad_norm * normed_flat, axis=-1, keepdims=True)
    grad_input = cot_flat.astype(jnp.float32) + scale_flat * (grad_norm - normed_flat * center)
    input_grad = grad_input.astype(jnp.bfloat16).reshape(samp_count, bin_count, width)
    return (input_grad, conv_grad)


def solution(mesh):
    return jax.shard_map(
        body,
        mesh=mesh,
        in_specs=(P("dp", "seq", None), P(None, "dp", "seq"), P("seq", "dp"), P("dp", "seq", None)),
        out_specs=(P("dp", "seq", None), P(None, "dp", "seq")),
        check_vma=False,
    )
```

```python
import functools

import jax
import jax.numpy as jnp
from jax import lax
from jax.experimental import pallas as pl
from jax.experimental.pallas import tpu as pltpu
from jax.sharding import Mesh
from jax.sharding import PartitionSpec as P

LANES = 128
X_PARTS, Y_PARTS, CORES = 4, 2, 2
GROUPS = 2
VMEM_BYTES = 40 * 1024 * 1024

EPSILON = 1e-06
GELU_SCALE = 0.7978845608028654
GELU_CUBIC = 0.044715


def gelu_tanh(values):
    return (
        0.5
        * values
        * (1.0 + jnp.tanh(GELU_SCALE * (values + GELU_CUBIC * values * values * values)))
    )


def gelu_slope(values):
    tangent = jnp.tanh(GELU_SCALE * (values + GELU_CUBIC * values * values * values))
    return 0.5 * (1.0 + tangent) + 0.5 * values * (1.0 - tangent * tangent) * GELU_SCALE * (
        1.0 + 3.0 * GELU_CUBIC * values * values
    )


def dot(left, right, left_dim, right_dim):
    return lax.dot_general(
        left, right, (((left_dim,), (right_dim,)), ((), ())), preferred_element_type=jnp.float32
    )


def normalize(values):
    floats = values.astype(jnp.float32)
    row_scale = lax.rsqrt(jnp.mean(floats * floats, axis=-1, keepdims=True) + EPSILON)
    return floats * row_scale, row_scale


def params():
    return pltpu.CompilerParams(vmem_limit_bytes=VMEM_BYTES)


def struct(shape, dtype):
    return jax.ShapeDtypeStruct(shape, dtype)


def cost(flops, nbytes):
    return pl.CostEstimate(flops=flops, bytes_accessed=nbytes, transcendentals=0)


def pack_kernel(conv_ref, point_ref, out_ref):
    taps, c_part, f_part = conv_ref.shape
    pieces = [conv_ref[tap].astype(jnp.float32) for tap in range(taps)]
    pieces.append(point_ref[...].astype(jnp.float32).T)
    pieces.append(jnp.zeros((c_part, LANES - (taps + 1) * f_part), jnp.float32))
    packed = jnp.concatenate(pieces, axis=1).astype(out_ref.dtype)
    out_ref[...] = jnp.broadcast_to(packed[None], out_ref.shape)


def pack(conv_weight, point_weight, peers):
    c_part = conv_weight.shape[1]
    return pl.pallas_call(
        pack_kernel,
        out_shape=struct((peers, c_part, LANES), conv_weight.dtype),
        compiler_params=params(),
        cost_estimate=cost(0, 2 * peers * c_part * LANES),
        name="pack",
    )(conv_weight, point_weight)


def by_tap_kernel(f_part, in_ref, *refs):
    out_refs = refs[-GROUPS:]
    taps = out_refs[0].shape[1]
    turned = [in_ref[y].astype(jnp.float32).T for y in range(Y_PARTS)]
    for tap in range(GROUPS * taps):
        rows = jnp.concatenate([t[tap * f_part : (tap + 1) * f_part] for t in turned], axis=0)
        out_ref = out_refs[tap // taps]
        for copy in range(X_PARTS):
            out_ref[copy, tap % taps] = rows.astype(out_ref.dtype)


def by_tap(gathered, f_part, taps, after):
    width = gathered.shape[1]
    return pl.pallas_call(
        functools.partial(by_tap_kernel, f_part),
        in_specs=[pl.BlockSpec(memory_space=pltpu.VMEM)]
        + [pl.BlockSpec(memory_space=pl.ANY)] * len(after),
        out_shape=[struct((X_PARTS, taps // GROUPS, Y_PARTS * f_part, width), gathered.dtype)]
        * GROUPS,
        compiler_params=params(),
        cost_estimate=cost(0, 4 * gathered.size * 2),
        name="by_tap",
    )(gathered, *after)


def by_channel_kernel(f_part, in_ref, out_ref):
    peers, taps, _, width = in_ref.shape
    total = [sum(in_ref[p, tap].astype(jnp.float32) for p in range(peers)) for tap in range(taps)]
    blank = jnp.zeros((LANES - taps * f_part, width), jnp.float32)
    for y in range(Y_PARTS):
        rows = [t[y * f_part : (y + 1) * f_part] for t in total] + [blank]
        out_ref[y] = jnp.concatenate(rows, axis=0).T.astype(out_ref.dtype)


def by_channel(parts, f_part):
    width = parts.shape[3]
    return pl.pallas_call(
        functools.partial(by_channel_kernel, f_part),
        out_shape=struct((Y_PARTS, width, LANES), parts.dtype),
        compiler_params=params(),
        cost_estimate=cost(0, 4 * parts.size),
        name="by_channel",
    )(parts)


def act_kernel(in_ref, out_ref):
    normed, _ = normalize(in_ref[...])
    out_ref[...] = gelu_tanh(normed).astype(out_ref.dtype)


def activate(inputs, block):
    samples, bins, width = inputs.shape
    rows = pl.BlockSpec((None, block, width), lambda s, i: (s, i, 0))
    return pl.pallas_call(
        act_kernel,
        grid=(samples, bins // block),
        in_specs=[rows],
        out_specs=rows,
        out_shape=struct(inputs.shape, inputs.dtype),
        compiler_params=params(),
        cost_estimate=cost(20 * inputs.size, 4 * inputs.size),
        name="activate",
    )(inputs)


def join_weights(own_refs, other_refs, joined, taps):
    each = own_refs[0].shape[1]
    for tap in range(taps):
        for side, refs in enumerate((own_refs, other_refs)):
            rows = refs[tap // each][:, tap % each].reshape(-1, joined.shape[2])
            joined[tap, pl.ds(side * rows.shape[0], rows.shape[0]), :] = rows


def forward_kernel(scale, samples, steps, *refs):
    acts_refs, cot_ref, refs = refs[:3], refs[3], refs[4:]
    own_w, other_w, refs = refs[:GROUPS], refs[GROUPS : 2 * GROUPS], refs[2 * GROUPS :]
    pre_ref, own_out, other_out, weights, acc = refs
    step = pl.program_id(0)

    @pl.when(step == 0)
    def _():
        join_weights(own_w, other_w, weights, 4)
        acc[...] = jnp.zeros_like(acc)

    for sample in range(samples):
        low, mid, high = [r[sample] for r in acts_refs]
        shifted_low = dot(low, weights[0], 1, 1).astype(jnp.bfloat16).astype(jnp.float32)
        shifted_high = dot(high, weights[2], 1, 1).astype(jnp.bfloat16).astype(jnp.float32)
        preact = shifted_low + dot(mid, weights[1], 1, 1) + shifted_high
        grad_inner = dot(cot_ref[sample], weights[3], 1, 1)
        grad_pre = (grad_inner * gelu_slope(preact)).astype(jnp.bfloat16)
        pre_ref[sample] = grad_pre
        for tap, acts in enumerate((low, mid, high)):
            acc[tap] += dot(grad_pre, acts, 0, 0)

    @pl.when(step == steps - 1)
    def _():
        half = acc.shape[1] // CORES
        for tap in range(3):
            own = acc[tap, pl.ds(0, half), :] * scale
            other = acc[tap, pl.ds(half, half), :] * scale
            own_out[:, tap] = own.reshape(own_out.shape[0], -1, own.shape[1])
            other_out[:, tap] = other.astype(jnp.bfloat16).reshape(
                other_out.shape[0], -1, own.shape[1]
            )


def forward(acts, cotangent, own_w, other_w, scale, block):
    samples, bins, width = cotangent.shape
    parts, _, f_rows, _ = own_w[0].shape
    hidden = CORES * parts * f_rows
    steps = bins // block
    rows = pl.BlockSpec((samples, block, width), lambda i: (0, i, 0))
    whole = pl.BlockSpec(own_w[0].shape, lambda i: (0, 0, 0, 0))
    half = (parts, 3, f_rows, width)
    half_spec = pl.BlockSpec(half, lambda i: (0, 0, 0, 0))
    return pl.pallas_call(
        functools.partial(forward_kernel, scale, samples, steps),
        grid=(steps,),
        in_specs=[rows] * 4 + [whole] * (2 * GROUPS),
        out_specs=[
            pl.BlockSpec((samples, block, hidden), lambda i: (0, i, 0)),
            half_spec,
            half_spec,
        ],
        out_shape=[
            struct((samples, bins, hidden), jnp.bfloat16),
            struct(half, jnp.float32),
            struct(half, jnp.bfloat16),
        ],
        scratch_shapes=[
            pltpu.VMEM((4, hidden, width), jnp.bfloat16),
            pltpu.VMEM((3, hidden, width), jnp.float32),
        ],
        compiler_params=params(),
        cost_estimate=cost(14 * samples * bins * width * hidden, 16 * samples * bins * width),
        name="forward",
    )(*acts, cotangent, *own_w, *other_w)


def backward_kernel(in_ref, cot_ref, up_ref, pre_ref, low_ref, *refs):
    own_w, other_w, (out_ref, weights) = refs[:GROUPS], refs[GROUPS:-2], refs[-2:]

    @pl.when(pl.program_id(0) == 0)
    def _():
        join_weights(own_w, other_w, weights, 3)

    for sample in range(in_ref.shape[0]):
        grad_act = (
            dot(up_ref[sample], weights[0], 1, 0)
            + dot(pre_ref[sample], weights[1], 1, 0)
            + dot(low_ref[sample], weights[2], 1, 0)
        )
        normed, row_scale = normalize(in_ref[sample])
        grad_norm = grad_act * gelu_slope(normed)
        center = jnp.mean(grad_norm * normed, axis=-1, keepdims=True)
        grad = cot_ref[sample].astype(jnp.float32) + row_scale * (grad_norm - normed * center)
        out_ref[sample] = grad.astype(out_ref.dtype)


def backward(inputs, cotangent, grad_upper, grad_pre, grad_lower, own_w, other_w, block):
    samples, bins, width = inputs.shape
    hidden = grad_pre.shape[2]
    wide = pl.BlockSpec((samples, block, width), lambda i: (0, i, 0))
    narrow = pl.BlockSpec((samples, block, hidden), lambda i: (0, i, 0))
    whole = pl.BlockSpec(own_w[0].shape, lambda i: (0, 0, 0, 0))
    return pl.pallas_call(
        backward_kernel,
        grid=(bins // block,),
        in_specs=[wide, wide, narrow, narrow, narrow] + [whole] * (2 * GROUPS),
        out_specs=wide,
        out_shape=struct(inputs.shape, inputs.dtype),
        scratch_shapes=[pltpu.VMEM((3, hidden, width), jnp.bfloat16)],
        compiler_params=params(),
        cost_estimate=cost(6 * samples * bins * width * hidden, 16 * samples * bins * width),
        name="backward",
    )(inputs, cotangent, grad_upper, grad_pre, grad_lower, *own_w, *other_w)


def shifted(array, by):
    count = X_PARTS * Y_PARTS
    pairs = [(i, i + by) for i in range(count) if 0 <= i + by < count]
    return lax.ppermute(array, ("x", "yh"), pairs)


def other_core(array):
    return lax.ppermute(array, "core", [(0, 1), (1, 0)])


def body(inputs, conv_weight, point_weight, cotangent):
    samples, bins, width = inputs.shape
    taps, c_part, f_part = conv_weight.shape
    n_dp = lax.axis_size("dp")
    devices = n_dp * X_PARTS * Y_PARTS * CORES
    grad_scale = float(samples * bins * devices) ** (-0.5)

    packed = pack(conv_weight, point_weight, Y_PARTS * n_dp)
    gathered = lax.all_to_all(packed, ("yh", "dp"), 0, 0).reshape(Y_PARTS, width, LANES)

    acted = activate(inputs, 256)
    acts = (shifted(acted, 1), acted, shifted(acted, -1))

    copies = by_tap(gathered, f_part, taps + 1, [acted])
    own_w = [lax.all_to_all(part, "x", 0, 0) for part in copies]
    other_w = [other_core(part) for part in own_w]

    grad_pre, own, other = forward(acts, cotangent, own_w, other_w, grad_scale, 128)

    grad_upper = shifted(grad_pre, -1)
    grad_lower = shifted(grad_pre, 1)

    pair = (own + other_core(other).astype(jnp.float32)).astype(jnp.bfloat16)
    parts = lax.all_to_all(pair, "x", 0, 0)
    sums = by_channel(parts, f_part).reshape(Y_PARTS * n_dp, c_part, LANES)
    pieces = lax.all_to_all(sums, ("yh", "dp"), 0, 0)
    total = jnp.sum(pieces.astype(jnp.float32), axis=0)
    conv_grad = jnp.stack([total[:, t * f_part : (t + 1) * f_part] for t in range(taps)], axis=0)

    input_grad = backward(
        inputs, cotangent, grad_upper, grad_pre, grad_lower, own_w, other_w, 128
    )
    return (input_grad, conv_grad)


def solution(mesh):
    n_dp = mesh.shape["dp"]
    fine = Mesh(
        mesh.devices.reshape(n_dp, X_PARTS, Y_PARTS, CORES), ("dp", "x", "yh", "core")
    )
    seq = ("x", "yh", "core")
    return jax.shard_map(
        body,
        mesh=fine,
        in_specs=(P("dp", seq, None), P(None, "dp", seq), P(seq, "dp"), P("dp", seq, None)),
        out_specs=(P("dp", seq, None), P(None, "dp", seq)),
        check_vma=False,
    )
```

```python
import functools

import jax
import jax.numpy as jnp
from jax import lax
from jax.experimental import pallas as pl
from jax.experimental.pallas import tpu as pltpu
from jax.sharding import Mesh
from jax.sharding import PartitionSpec as P

LANES = 128
X_PARTS, Y_PARTS, CORES = 4, 2, 2
GROUPS = 2
MIB = 1024 * 1024

EPSILON = 1e-06
GELU_SCALE = 0.7978845608028654
GELU_CUBIC = 0.044715


def gelu_tanh(values):
    return (
        0.5
        * values
        * (1.0 + jnp.tanh(GELU_SCALE * (values + GELU_CUBIC * values * values * values)))
    )


def gelu_slope(values):
    tangent = jnp.tanh(GELU_SCALE * (values + GELU_CUBIC * values * values * values))
    return 0.5 * (1.0 + tangent) + 0.5 * values * (1.0 - tangent * tangent) * GELU_SCALE * (
        1.0 + 3.0 * GELU_CUBIC * values * values
    )


def dot(left, right, left_dim, right_dim):
    return lax.dot_general(
        left, right, (((left_dim,), (right_dim,)), ((), ())), preferred_element_type=jnp.float32
    )


def normalize(values):
    floats = values.astype(jnp.float32)
    row_scale = lax.rsqrt(jnp.mean(floats * floats, axis=-1, keepdims=True) + EPSILON)
    return floats * row_scale, row_scale


def params(mib):
    return pltpu.CompilerParams(vmem_limit_bytes=mib * MIB)


def struct(shape, dtype):
    return jax.ShapeDtypeStruct(shape, dtype)


def cost(flops, nbytes):
    return pl.CostEstimate(flops=flops, bytes_accessed=nbytes, transcendentals=0)


ANYWHERE = pl.BlockSpec(memory_space=pl.ANY)
IN_VMEM = pl.BlockSpec(memory_space=pltpu.VMEM)


def pack_kernel(conv_ref, point_ref, *refs):
    out_ref = refs[-1]
    taps, c_part, f_part = conv_ref.shape
    pieces = [conv_ref[tap].astype(jnp.float32) for tap in range(taps)]
    pieces.append(point_ref[...].astype(jnp.float32).T)
    pieces.append(jnp.zeros((c_part, LANES - (taps + 1) * f_part), jnp.float32))
    packed = jnp.concatenate(pieces, axis=1).astype(out_ref.dtype)
    out_ref[...] = jnp.broadcast_to(packed[None], out_ref.shape)


def pack(conv_weight, point_weight, peers, after):
    c_part = conv_weight.shape[1]
    return pl.pallas_call(
        pack_kernel,
        in_specs=[IN_VMEM, IN_VMEM, ANYWHERE],
        out_shape=struct((peers, c_part, LANES), conv_weight.dtype),
        compiler_params=params(8),
        cost_estimate=cost(0, 2 * peers * c_part * LANES),
        name="pack",
    )(conv_weight, point_weight, after)


def by_tap_kernel(f_part, in_ref, *out_refs):
    taps = out_refs[0].shape[1]
    width = out_refs[0].shape[3]
    turned = []
    for y in range(Y_PARTS):
        rows = jnp.stack([in_ref[y, low].astype(jnp.float32) for low in range(Y_PARTS)], axis=1)
        turned.append(rows.reshape(width, LANES).T)
    for tap in range(GROUPS * taps):
        rows = jnp.concatenate([t[tap * f_part : (tap + 1) * f_part] for t in turned], axis=0)
        out_ref = out_refs[tap // taps]
        for copy in range(X_PARTS):
            out_ref[copy, tap % taps] = rows.astype(out_ref.dtype)


def by_tap(gathered, f_part, taps):
    width = gathered.shape[1] * gathered.shape[2] * gathered.shape[3]
    out = struct((X_PARTS, taps // GROUPS, Y_PARTS * f_part, width), gathered.dtype)
    return pl.pallas_call(
        functools.partial(by_tap_kernel, f_part),
        out_shape=[out] * GROUPS,
        compiler_params=params(16),
        cost_estimate=cost(0, 4 * gathered.size * 2),
        name="by_tap",
    )(gathered)


def by_channel_kernel(f_part, in_ref, out_ref):
    peers, taps, _, width = in_ref.shape
    depth, c_part = out_ref.shape[2:4]
    total = [sum(in_ref[p, tap].astype(jnp.float32) for p in range(peers)) for tap in range(taps)]
    blank = jnp.zeros((LANES - taps * f_part, width), jnp.float32)
    for y in range(Y_PARTS):
        rows = [t[y * f_part : (y + 1) * f_part] for t in total] + [blank]
        turned = jnp.concatenate(rows, axis=0).T.reshape(depth, Y_PARTS, c_part, LANES)
        for low in range(Y_PARTS):
            out_ref[y, low] = turned[:, low].astype(out_ref.dtype)


def by_channel(parts, f_part, depth):
    c_part = parts.shape[3] // (depth * Y_PARTS)
    return pl.pallas_call(
        functools.partial(by_channel_kernel, f_part),
        out_shape=struct((Y_PARTS, Y_PARTS, depth, c_part, LANES), parts.dtype),
        compiler_params=params(16),
        cost_estimate=cost(0, 4 * parts.size),
        name="by_channel",
    )(parts)


def add_kernel(in_ref, *refs):
    out_ref = refs[-1]
    total = sum(in_ref[p].astype(jnp.float32) for p in range(in_ref.shape[0]))
    out_ref[...] = total.astype(out_ref.dtype)


def add_parts(parts, after):
    return pl.pallas_call(
        add_kernel,
        in_specs=[IN_VMEM] + [ANYWHERE] * len(after),
        out_shape=struct(parts.shape[1:], parts.dtype),
        compiler_params=params(8),
        cost_estimate=cost(0, 4 * parts.size),
        name="add_parts",
    )(parts, *after)


def finish_kernel(in_ref, out_ref):
    taps, _, f_part = out_ref.shape
    total = sum(in_ref[p].astype(jnp.float32) for p in range(in_ref.shape[0]))
    for tap in range(taps):
        out_ref[tap] = total[:, tap * f_part : (tap + 1) * f_part]


def finish(pieces, taps, f_part):
    return pl.pallas_call(
        finish_kernel,
        out_shape=struct((taps, pieces.shape[1], f_part), jnp.float32),
        compiler_params=params(8),
        cost_estimate=cost(0, 4 * pieces.size),
        name="finish",
    )(pieces)


def act_kernel(in_ref, out_ref):
    normed, _ = normalize(in_ref[...])
    out_ref[...] = gelu_tanh(normed).astype(out_ref.dtype)


def activate(inputs, block):
    samples, bins, width = inputs.shape
    rows = pl.BlockSpec((None, block, width), lambda s, i: (s, i, 0))
    return pl.pallas_call(
        act_kernel,
        grid=(samples, bins // block),
        in_specs=[rows],
        out_specs=rows,
        out_shape=struct(inputs.shape, inputs.dtype),
        compiler_params=params(8),
        cost_estimate=cost(20 * inputs.size, 4 * inputs.size),
        name="activate",
    )(inputs)


def join_weights(own_refs, other_refs, joined, taps):
    each = own_refs[0].shape[1]
    for tap in range(taps):
        for side, refs in enumerate((own_refs, other_refs)):
            rows = refs[tap // each][:, tap % each].reshape(-1, joined.shape[2])
            joined[tap, pl.ds(side * rows.shape[0], rows.shape[0]), :] = rows


def forward_kernel(scale, *refs):
    acts_refs, cot_ref, refs = refs[:3], refs[3], refs[4:]
    own_w, other_w, refs = refs[:GROUPS], refs[GROUPS : 2 * GROUPS], refs[2 * GROUPS :]
    pre_ref, own_out, other_out, weights, turned = refs
    samples, bins, width = cot_ref.shape
    half = weights.shape[1] // CORES
    join_weights(own_w, other_w, weights, 4)
    for sample in range(samples):
        low, mid, high = [r[sample] for r in acts_refs]
        shifted_low = dot(low, weights[0], 1, 1).astype(jnp.bfloat16).astype(jnp.float32)
        shifted_high = dot(high, weights[2], 1, 1).astype(jnp.bfloat16).astype(jnp.float32)
        preact = shifted_low + dot(mid, weights[1], 1, 1) + shifted_high
        grad_inner = dot(cot_ref[sample], weights[3], 1, 1)
        grad_pre = grad_inner * gelu_slope(preact)
        pre_ref[sample] = grad_pre.astype(jnp.bfloat16)
        turned[:, pl.ds(sample * bins, bins)] = grad_pre.T.astype(jnp.bfloat16)
    for tap, acts_ref in enumerate(acts_refs):
        acts = acts_ref[...].reshape(samples * bins, width)
        term = dot(turned[...], acts, 1, 0) * scale
        own_out[:, tap] = term[:half].reshape(own_out.shape[0], -1, width)
        other = term[half:].astype(jnp.bfloat16)
        other_out[:, tap] = other.reshape(other_out.shape[0], -1, width)


def forward(acts, cotangent, own_w, other_w, scale):
    samples, bins, width = cotangent.shape
    parts, _, f_rows, _ = own_w[0].shape
    hidden = CORES * parts * f_rows
    half = (parts, 3, f_rows, width)
    return pl.pallas_call(
        functools.partial(forward_kernel, scale),
        out_shape=[
            struct((samples, bins, hidden), jnp.bfloat16),
            struct(half, jnp.float32),
            struct(half, jnp.bfloat16),
        ],
        scratch_shapes=[
            pltpu.VMEM((4, hidden, width), jnp.bfloat16),
            pltpu.VMEM((hidden, samples * bins), jnp.bfloat16),
        ],
        compiler_params=params(24),
        cost_estimate=cost(14 * samples * bins * width * hidden, 16 * samples * bins * width),
        name="forward",
    )(*acts, cotangent, *own_w, *other_w)


def backward_kernel(in_ref, cot_ref, up_ref, pre_ref, low_ref, *refs):
    own_w, other_w, (out_ref, weights) = refs[:GROUPS], refs[GROUPS:-2], refs[-2:]

    @pl.when(pl.program_id(0) == 0)
    def _():
        join_weights(own_w, other_w, weights, 3)

    for sample in range(in_ref.shape[0]):
        grad_act = (
            dot(up_ref[sample], weights[0], 1, 0)
            + dot(pre_ref[sample], weights[1], 1, 0)
            + dot(low_ref[sample], weights[2], 1, 0)
        )
        normed, row_scale = normalize(in_ref[sample])
        grad_norm = grad_act * gelu_slope(normed)
        center = jnp.mean(grad_norm * normed, axis=-1, keepdims=True)
        grad = cot_ref[sample].astype(jnp.float32) + row_scale * (grad_norm - normed * center)
        out_ref[sample] = grad.astype(out_ref.dtype)


def backward(inputs, cotangent, grad_upper, grad_pre, grad_lower, own_w, other_w, block):
    samples, bins, width = inputs.shape
    hidden = grad_pre.shape[2]
    wide = pl.BlockSpec((samples, block, width), lambda i: (0, i, 0))
    narrow = pl.BlockSpec((samples, block, hidden), lambda i: (0, i, 0))
    whole = pl.BlockSpec(
        own_w[0].shape, lambda i: (0, 0, 0, 0), pipeline_mode=pl.Buffered(1)
    )
    return pl.pallas_call(
        backward_kernel,
        grid=(bins // block,),
        in_specs=[wide, wide, narrow, narrow, narrow] + [whole] * (2 * GROUPS),
        out_specs=wide,
        out_shape=struct(inputs.shape, inputs.dtype),
        scratch_shapes=[pltpu.VMEM((3, hidden, width), jnp.bfloat16)],
        compiler_params=params(24),
        cost_estimate=cost(6 * samples * bins * width * hidden, 16 * samples * bins * width),
        name="backward",
    )(inputs, cotangent, grad_upper, grad_pre, grad_lower, *own_w, *other_w)


def shifted(array, by):
    count = X_PARTS * Y_PARTS
    pairs = [(i, i + by) for i in range(count) if 0 <= i + by < count]
    return lax.ppermute(array, ("x", "yh"), pairs)


def other_core(array):
    return lax.ppermute(array, "core", [(0, 1), (1, 0)])


def body(inputs, conv_weight, point_weight, cotangent):
    samples, bins, width = inputs.shape
    taps, c_part, f_part = conv_weight.shape
    depth = lax.axis_size("z")
    devices = depth * Y_PARTS * X_PARTS * Y_PARTS * CORES
    grad_scale = float(samples * bins * devices) ** (-0.5)

    acted = activate(inputs, 256)
    acts = (shifted(acted, 1), acted, shifted(acted, -1))

    along_z = lax.all_to_all(pack(conv_weight, point_weight, depth, acted), "z", 0, 0)
    copies = jnp.broadcast_to(along_z[None], (Y_PARTS * Y_PARTS,) + along_z.shape)
    gathered = lax.all_to_all(copies, ("yh", "yl"), 0, 0)
    gathered = gathered.reshape(Y_PARTS, Y_PARTS, depth, c_part, LANES)
    own_w = [lax.all_to_all(part, "x", 0, 0) for part in by_tap(gathered, f_part, taps + 1)]
    other_w = [other_core(part) for part in own_w]

    grad_pre, own, other = forward(acts, cotangent, own_w, other_w, grad_scale)

    grad_upper = shifted(grad_pre, -1)
    grad_lower = shifted(grad_pre, 1)

    pair = (own + other_core(other).astype(jnp.float32)).astype(jnp.bfloat16)
    sums = by_channel(lax.all_to_all(pair, "x", 0, 0), f_part, depth)
    sums = sums.reshape(Y_PARTS * Y_PARTS, depth, c_part, LANES)
    sums = add_parts(lax.all_to_all(sums, ("yh", "yl"), 0, 0), (grad_upper, grad_lower))
    conv_grad = finish(lax.all_to_all(sums, "z", 0, 0), taps, f_part)

    input_grad = backward(
        inputs, cotangent, grad_upper, grad_pre, grad_lower, own_w, other_w, 256
    )
    return (input_grad, conv_grad)


def solution(mesh):
    depth = mesh.shape["dp"] // Y_PARTS
    fine = Mesh(
        mesh.devices.reshape(depth, Y_PARTS, X_PARTS, Y_PARTS, CORES),
        ("z", "yl", "x", "yh", "core"),
    )
    dp, seq = ("z", "yl"), ("x", "yh", "core")
    return jax.shard_map(
        body,
        mesh=fine,
        in_specs=(P(dp, seq, None), P(None, dp, seq), P(seq, dp), P(dp, seq, None)),
        out_specs=(P(dp, seq, None), P(None, dp, seq)),
        check_vma=False,
    )
```

```python
import functools

import jax
import jax.numpy as jnp
from jax import lax
from jax.experimental import pallas as pl
from jax.experimental.pallas import tpu as pltpu
from jax.sharding import Mesh
from jax.sharding import PartitionSpec as P

LANES = 128
X_PARTS, Y_PARTS, Z_PARTS, CORES = 4, 2, 4, 2
GROUPS = 1
MIB = 1024 * 1024

EPSILON = 1e-06
GELU_SCALE = 0.7978845608028654
GELU_CUBIC = 0.044715


def gelu_tanh(values):
    return (
        0.5
        * values
        * (1.0 + jnp.tanh(GELU_SCALE * (values + GELU_CUBIC * values * values * values)))
    )


def gelu_slope(values):
    tangent = jnp.tanh(GELU_SCALE * (values + GELU_CUBIC * values * values * values))
    return 0.5 * (1.0 + tangent) + 0.5 * values * (1.0 - tangent * tangent) * GELU_SCALE * (
        1.0 + 3.0 * GELU_CUBIC * values * values
    )


def dot(left, right, left_dim, right_dim):
    return lax.dot_general(
        left, right, (((left_dim,), (right_dim,)), ((), ())), preferred_element_type=jnp.float32
    )


def normalize(values):
    floats = values.astype(jnp.float32)
    row_scale = lax.rsqrt(jnp.mean(floats * floats, axis=-1, keepdims=True) + EPSILON)
    return floats * row_scale, row_scale


def params(mib):
    return pltpu.CompilerParams(vmem_limit_bytes=mib * MIB)


def struct(shape, dtype):
    return jax.ShapeDtypeStruct(shape, dtype)


def cost(flops, nbytes):
    return pl.CostEstimate(flops=flops, bytes_accessed=nbytes, transcendentals=0)


ANYWHERE = pl.BlockSpec(memory_space=pl.ANY)
IN_VMEM = pl.BlockSpec(memory_space=pltpu.VMEM)


def pack_kernel(conv_ref, point_ref, out_ref):
    taps, c_part, f_part = conv_ref.shape
    pieces = [conv_ref[tap].astype(jnp.float32) for tap in range(taps)]
    pieces.append(point_ref[...].astype(jnp.float32).T)
    pieces.append(jnp.zeros((c_part, LANES - (taps + 1) * f_part), jnp.float32))
    packed = jnp.concatenate(pieces, axis=1).astype(out_ref.dtype)
    out_ref[...] = jnp.broadcast_to(packed[None], out_ref.shape)


def pack(conv_weight, point_weight, peers):
    c_part = conv_weight.shape[1]
    return pl.pallas_call(
        pack_kernel,
        out_shape=struct((peers, c_part, LANES), conv_weight.dtype),
        compiler_params=params(8),
        cost_estimate=cost(0, 2 * peers * c_part * LANES),
        name="pack",
    )(conv_weight, point_weight)


def assemble_kernel(f_part, taps, in_ref, _, out_ref):
    blocks = in_ref.shape[0] // Y_PARTS
    for low in range(Y_PARTS):
        pieces = [in_ref[Y_PARTS * block + low].astype(jnp.float32) for block in range(blocks)]
        rows = jnp.concatenate(
            [
                piece[:, tap * f_part : (tap + 1) * f_part]
                for tap in range(taps)
                for piece in pieces
            ],
            axis=1,
        )
        span = rows.shape[0]
        for copy in range(Z_PARTS):
            out_ref[copy, pl.ds(low * span, span), :] = rows.astype(out_ref.dtype)


def assemble(gathered, f_part, taps, after):
    peers, c_part, _ = gathered.shape
    lanes = peers // Y_PARTS * taps * f_part
    return pl.pallas_call(
        functools.partial(assemble_kernel, f_part, taps),
        in_specs=[IN_VMEM, ANYWHERE],
        out_shape=struct((Z_PARTS, Y_PARTS * c_part, lanes), gathered.dtype),
        compiler_params=params(8),
        cost_estimate=cost(0, 4 * gathered.size * 2),
        name="assemble",
    )(gathered, after)


def turn_kernel(f_part, own_ref, other_ref, out_ref):
    taps, rows, width = own_ref.shape
    far, near, span, lanes = out_ref.shape[1], out_ref.shape[0], *out_ref.shape[2:]
    total = [own_ref[tap] + other_ref[tap].astype(jnp.float32) for tap in range(taps)]
    blocks = [
        total[tap][block * f_part : (block + 1) * f_part]
        for block in range(rows // f_part)
        for tap in range(taps)
    ]
    blocks.append(jnp.zeros((lanes - taps * rows, width), jnp.float32))
    turned = jnp.concatenate(blocks, axis=0).T
    for zh in range(far):
        for zl in range(near):
            first = (zh * near + zl) * span
            out_ref[zl, zh] = turned[first : first + span].astype(out_ref.dtype)


def turn(own, other, f_part, depth):
    taps, rows, width = own.shape
    lanes = -(-taps * rows // LANES) * LANES
    out = (Z_PARTS, depth // Z_PARTS, width // depth, lanes)
    return pl.pallas_call(
        functools.partial(turn_kernel, f_part),
        out_shape=struct(out, jnp.bfloat16),
        compiler_params=params(16),
        cost_estimate=cost(0, 8 * own.size),
        name="turn",
    )(own, other)


def split_kernel(lanes, in_ref, *refs):
    out_ref = refs[-1]
    total = sum(in_ref[p].astype(jnp.float32) for p in range(in_ref.shape[0]))
    span = out_ref.shape[1]
    blank = jnp.zeros((span, LANES - lanes), jnp.float32)
    for block in range(out_ref.shape[0] // Y_PARTS):
        for low in range(Y_PARTS):
            part = total[low * span : (low + 1) * span, block * lanes : (block + 1) * lanes]
            part = jnp.concatenate([part, blank], axis=1)
            out_ref[Y_PARTS * block + low] = part.astype(out_ref.dtype)


def split(parts, lanes, blocks, after):
    return pl.pallas_call(
        functools.partial(split_kernel, lanes),
        in_specs=[IN_VMEM] + [ANYWHERE] * len(after),
        out_shape=struct((blocks * Y_PARTS, parts.shape[1] // Y_PARTS, LANES), parts.dtype),
        compiler_params=params(8),
        cost_estimate=cost(0, 4 * parts.size),
        name="split",
    )(parts, *after)


def add_kernel(in_ref, out_ref):
    total = sum(in_ref[p].astype(jnp.float32) for p in range(in_ref.shape[0]))
    out_ref[...] = total.astype(out_ref.dtype)


def add_parts(parts):
    return pl.pallas_call(
        add_kernel,
        out_shape=struct(parts.shape[1:], parts.dtype),
        compiler_params=params(8),
        cost_estimate=cost(0, 4 * parts.size),
        name="add_parts",
    )(parts)


def finish_kernel(in_ref, out_ref):
    taps, _, f_part = out_ref.shape
    total = sum(in_ref[p].astype(jnp.float32) for p in range(in_ref.shape[0]))
    for tap in range(taps):
        out_ref[tap] = total[:, tap * f_part : (tap + 1) * f_part]


def finish(pieces, taps, f_part):
    return pl.pallas_call(
        finish_kernel,
        out_shape=struct((taps, pieces.shape[1], f_part), jnp.float32),
        compiler_params=params(8),
        cost_estimate=cost(0, 4 * pieces.size),
        name="finish",
    )(pieces)


def act_kernel(in_ref, _, out_ref):
    normed, _ = normalize(in_ref[...])
    out_ref[...] = gelu_tanh(normed).astype(out_ref.dtype)


def activate(inputs, block, after):
    samples, bins, width = inputs.shape
    rows = pl.BlockSpec((None, block, width), lambda s, i: (s, i, 0))
    return pl.pallas_call(
        act_kernel,
        grid=(samples, bins // block),
        in_specs=[rows, ANYWHERE],
        out_specs=rows,
        out_shape=struct(inputs.shape, inputs.dtype),
        compiler_params=params(8),
        cost_estimate=cost(20 * inputs.size, 4 * inputs.size),
        name="activate",
    )(inputs, after)


def join_weights(own_refs, other_refs, joined, point):
    near, each, span, lanes = own_refs[0].shape
    half = lanes // 4
    for side, refs in enumerate((own_refs, other_refs)):
        for group, ref in enumerate(refs):
            for zl in range(near):
                for part in range(each):
                    zh = group * each + part
                    rows = pl.ds((zh * near + zl) * span, span)
                    block = ref[zl, part]
                    for tap in range(4):
                        piece = block[:, tap * half : (tap + 1) * half]
                        if tap < 3:
                            joined[tap, rows, side * half : (side + 1) * half] = piece
                        else:
                            point[rows, side * half : (side + 1) * half] = piece


def forward_kernel(scale, *refs):
    acts_refs, cot_ref, refs = refs[:3], refs[3], refs[4:]
    own_w, other_w, refs = refs[:GROUPS], refs[GROUPS : 2 * GROUPS], refs[2 * GROUPS :]
    pre_ref, own_out, other_out, weights, point, turned = refs
    samples, bins, width = cot_ref.shape
    half = weights.shape[2] // CORES
    join_weights(own_w, other_w, weights, point)
    for sample in range(samples):
        low, mid, high = [r[sample] for r in acts_refs]
        shifted_low = dot(low, weights[0], 1, 0).astype(jnp.bfloat16).astype(jnp.float32)
        shifted_high = dot(high, weights[2], 1, 0).astype(jnp.bfloat16).astype(jnp.float32)
        preact = shifted_low + dot(mid, weights[1], 1, 0) + shifted_high
        grad_inner = dot(cot_ref[sample], point[...], 1, 0)
        grad_pre = grad_inner * gelu_slope(preact)
        pre_ref[sample] = grad_pre.astype(jnp.bfloat16)
        turned[:, pl.ds(sample * bins, bins)] = grad_pre.T.astype(jnp.bfloat16)
    for tap, acts_ref in enumerate(acts_refs):
        acts = acts_ref[...].reshape(samples * bins, width)
        term = dot(turned[...], acts, 1, 0) * scale
        own_out[tap] = term[:half]
        other_out[tap] = term[half:].astype(jnp.bfloat16)


def forward(acts, cotangent, own_w, other_w, scale):
    samples, bins, width = cotangent.shape
    hidden = CORES * own_w[0].shape[3] // 4
    half = (3, hidden // CORES, width)
    return pl.pallas_call(
        functools.partial(forward_kernel, scale),
        out_shape=[
            struct((samples, bins, hidden), jnp.bfloat16),
            struct(half, jnp.float32),
            struct(half, jnp.bfloat16),
            struct((3, width, hidden), jnp.bfloat16),
        ],
        scratch_shapes=[
            pltpu.VMEM((width, hidden), jnp.bfloat16),
            pltpu.VMEM((hidden, samples * bins), jnp.bfloat16),
        ],
        compiler_params=params(24),
        cost_estimate=cost(14 * samples * bins * width * hidden, 16 * samples * bins * width),
        name="forward",
    )(*acts, cotangent, *own_w, *other_w)


def backward_kernel(in_ref, cot_ref, up_ref, pre_ref, low_ref, weights, out_ref):
    for sample in range(in_ref.shape[0]):
        grad_act = (
            dot(up_ref[sample], weights[0], 1, 1)
            + dot(pre_ref[sample], weights[1], 1, 1)
            + dot(low_ref[sample], weights[2], 1, 1)
        )
        normed, row_scale = normalize(in_ref[sample])
        grad_norm = grad_act * gelu_slope(normed)
        center = jnp.mean(grad_norm * normed, axis=-1, keepdims=True)
        grad = cot_ref[sample].astype(jnp.float32) + row_scale * (grad_norm - normed * center)
        out_ref[sample] = grad.astype(out_ref.dtype)


def backward(inputs, cotangent, grad_upper, grad_pre, grad_lower, weights, block):
    samples, bins, width = inputs.shape
    hidden = grad_pre.shape[2]
    wide = pl.BlockSpec((samples, block, width), lambda i: (0, i, 0))
    narrow = pl.BlockSpec((samples, block, hidden), lambda i: (0, i, 0))
    whole = pl.BlockSpec(weights.shape, lambda i: (0, 0, 0), pipeline_mode=pl.Buffered(1))
    return pl.pallas_call(
        backward_kernel,
        grid=(bins // block,),
        in_specs=[wide, wide, narrow, narrow, narrow, whole],
        out_specs=wide,
        out_shape=struct(inputs.shape, inputs.dtype),
        compiler_params=params(24),
        cost_estimate=cost(6 * samples * bins * width * hidden, 16 * samples * bins * width),
        name="backward",
    )(inputs, cotangent, grad_upper, grad_pre, grad_lower, weights)


def shifted(array, by):
    count = X_PARTS * Y_PARTS
    pairs = [(i, i + by) for i in range(count) if 0 <= i + by < count]
    return lax.ppermute(array, ("x", "yh"), pairs)


def other_core(array):
    return lax.ppermute(array, "core", [(0, 1), (1, 0)])


def body(inputs, conv_weight, point_weight, cotangent):
    samples, bins, width = inputs.shape
    taps, c_part, f_part = conv_weight.shape
    near, far = lax.axis_size("zl"), lax.axis_size("zh")
    depth = near * far
    blocks = X_PARTS * Y_PARTS
    devices = depth * Y_PARTS * blocks * CORES
    grad_scale = float(samples * bins * devices) ** (-0.5)
    plane = ("x", "yh", "yl")

    packed = pack(conv_weight, point_weight, blocks * Y_PARTS)
    pieces = lax.all_to_all(packed, plane, 0, 0)

    acted = activate(inputs, 256, pieces)
    acts = (shifted(acted, 1), acted, shifted(acted, -1))

    def along_z(spread):
        part = lax.all_to_all(spread, "zh", 0, 0)
        part = lax.all_to_all(jnp.broadcast_to(part[None], (near,) + part.shape), "zl", 0, 0)
        return part, other_core(part)

    def nothing(spread):
        blank = jnp.zeros((near,) + spread.shape, spread.dtype)
        return blank, blank

    spread = assemble(pieces, f_part, taps + 1, acted)[:far]
    own_w, other_w = lax.cond(lax.axis_index("x") < X_PARTS, along_z, nothing, spread)

    grad_pre, own, other, weights = forward(acts, cotangent, [own_w], [other_w], grad_scale)

    grad_upper = shifted(grad_pre, -1)
    grad_lower = shifted(grad_pre, 1)

    sums = lax.all_to_all(turn(own, other_core(other), f_part, depth), "zl", 0, 0)
    sums = lax.all_to_all(add_parts(sums), "zh", 0, 0)
    sums = split(sums, taps * f_part, blocks, (grad_upper, grad_lower))
    conv_grad = finish(lax.all_to_all(sums, plane, 0, 0), taps, f_part)

    input_grad = backward(inputs, cotangent, grad_upper, grad_pre, grad_lower, weights, 256)
    return (input_grad, conv_grad)


def solution(mesh):
    depth = mesh.shape["dp"] // Y_PARTS
    fine = Mesh(
        mesh.devices.reshape(depth // Z_PARTS, Z_PARTS, Y_PARTS, X_PARTS, Y_PARTS, CORES),
        ("zh", "zl", "yl", "x", "yh", "core"),
    )
    dp, seq = ("zh", "zl", "yl"), ("x", "yh", "core")
    return jax.shard_map(
        body,
        mesh=fine,
        in_specs=(P(dp, seq, None), P(None, dp, seq), P(seq, dp), P(dp, seq, None)),
        out_specs=(P(dp, seq, None), P(None, dp, seq)),
        check_vma=False,
    )
```

```python
import functools

import jax
import jax.numpy as jnp
from jax import lax
from jax.experimental import pallas as pl
from jax.experimental.pallas import tpu as pltpu
from jax.sharding import Mesh
from jax.sharding import PartitionSpec as P

LANES = 128
X_PARTS, Y_PARTS, Z_PARTS, CORES = 4, 2, 4, 2
MIB = 1024 * 1024

EPSILON = 1e-06
GELU_SCALE = 0.7978845608028654
GELU_CUBIC = 0.044715


def gelu_tanh(values):
    return (
        0.5
        * values
        * (1.0 + jnp.tanh(GELU_SCALE * (values + GELU_CUBIC * values * values * values)))
    )


def gelu_slope(values):
    tangent = jnp.tanh(GELU_SCALE * (values + GELU_CUBIC * values * values * values))
    return 0.5 * (1.0 + tangent) + 0.5 * values * (1.0 - tangent * tangent) * GELU_SCALE * (
        1.0 + 3.0 * GELU_CUBIC * values * values
    )


def dot(left, right, left_dim, right_dim):
    return lax.dot_general(
        left, right, (((left_dim,), (right_dim,)), ((), ())), preferred_element_type=jnp.float32
    )


def normalize(values):
    floats = values.astype(jnp.float32)
    row_scale = lax.rsqrt(jnp.mean(floats * floats, axis=-1, keepdims=True) + EPSILON)
    return floats * row_scale, row_scale


def params(mib):
    return pltpu.CompilerParams(vmem_limit_bytes=mib * MIB)


def struct(shape, dtype):
    return jax.ShapeDtypeStruct(shape, dtype)


def cost(flops, nbytes):
    return pl.CostEstimate(flops=flops, bytes_accessed=nbytes, transcendentals=0)


ANYWHERE = pl.BlockSpec(memory_space=pl.ANY)
IN_VMEM = pl.BlockSpec(memory_space=pltpu.VMEM)
IN_HBM = pl.BlockSpec(memory_space=pltpu.HBM)
IN_SMEM = pl.BlockSpec(memory_space=pltpu.SMEM)


def in_hbm(array):
    return pltpu.with_memory_space_constraint(array, pltpu.HBM)


def once_kernel(in_ref, *refs):
    refs[-1][...] = in_ref[...]


def once(array, *after):
    return pl.pallas_call(
        once_kernel,
        in_specs=[IN_VMEM] + [ANYWHERE] * len(after),
        out_shape=struct(array.shape, array.dtype),
        compiler_params=params(8),
        cost_estimate=cost(0, 4 * array.size),
        name="once",
    )(array, *after)


def held(stage, *args):
    def blank(*args):
        return jnp.zeros(out.shape, out.dtype)

    out = jax.eval_shape(stage, *args)
    return lax.cond(lax.axis_index("x") < X_PARTS, stage, blank, *args)


def pack_kernel(conv_ref, point_ref, out_ref):
    taps, c_part, f_part = conv_ref.shape
    pieces = [conv_ref[tap].astype(jnp.float32) for tap in range(taps)]
    pieces.append(point_ref[...].astype(jnp.float32).T)
    pieces.append(jnp.zeros((c_part, LANES - (taps + 1) * f_part), jnp.float32))
    packed = jnp.concatenate(pieces, axis=1).astype(out_ref.dtype)
    out_ref[...] = jnp.broadcast_to(packed[None], out_ref.shape)


def pack(conv_weight, point_weight, peers):
    c_part = conv_weight.shape[1]
    return pl.pallas_call(
        pack_kernel,
        out_shape=struct((peers, c_part, LANES), conv_weight.dtype),
        compiler_params=params(8),
        cost_estimate=cost(0, 2 * peers * c_part * LANES),
        name="pack",
    )(conv_weight, point_weight)


def assemble_kernel(f_part, taps, in_ref, out_ref):
    blocks = in_ref.shape[0] // Y_PARTS
    for low in range(Y_PARTS):
        pieces = [in_ref[Y_PARTS * block + low].astype(jnp.float32) for block in range(blocks)]
        rows = jnp.concatenate(
            [
                piece[:, tap * f_part : (tap + 1) * f_part]
                for tap in range(taps)
                for piece in pieces
            ],
            axis=1,
        )
        span = rows.shape[0]
        for copy in range(Z_PARTS):
            out_ref[copy, pl.ds(low * span, span), :] = rows.astype(out_ref.dtype)


def assemble(gathered, f_part, taps):
    peers, c_part, _ = gathered.shape
    lanes = peers // Y_PARTS * taps * f_part
    return pl.pallas_call(
        functools.partial(assemble_kernel, f_part, taps),
        out_shape=struct((Z_PARTS, Y_PARTS * c_part, lanes), gathered.dtype),
        compiler_params=params(8),
        cost_estimate=cost(0, 4 * gathered.size * 2),
        name="assemble",
    )(gathered)


def by_channel_kernel(f_part, in_ref, out_ref):
    peers, taps, _, width = in_ref.shape
    depth, c_part = out_ref.shape[0], out_ref.shape[3]
    total = [sum(in_ref[p, tap].astype(jnp.float32) for p in range(peers)) for tap in range(taps)]
    blank = jnp.zeros((LANES - taps * f_part, width), jnp.float32)
    for y in range(Y_PARTS):
        rows = [t[y * f_part : (y + 1) * f_part] for t in total] + [blank]
        turned = jnp.concatenate(rows, axis=0).T.reshape(depth, Y_PARTS, c_part, LANES)
        for low in range(Y_PARTS):
            out_ref[:, y, low] = turned[:, low].astype(out_ref.dtype)


def by_channel(parts, f_part, depth):
    c_part = parts.shape[3] // (depth * Y_PARTS)
    return pl.pallas_call(
        functools.partial(by_channel_kernel, f_part),
        out_shape=struct((depth, Y_PARTS, Y_PARTS, c_part, LANES), parts.dtype),
        compiler_params=params(16),
        cost_estimate=cost(0, 4 * parts.size),
        name="by_channel",
    )(parts)


def add_kernel(in_ref, out_ref):
    total = sum(in_ref[p].astype(jnp.float32) for p in range(in_ref.shape[0]))
    out_ref[...] = total.astype(out_ref.dtype)


def add_parts(parts):
    return pl.pallas_call(
        add_kernel,
        out_shape=struct(parts.shape[1:], parts.dtype),
        compiler_params=params(8),
        cost_estimate=cost(0, 4 * parts.size),
        name="add_parts",
    )(parts)


def finish_kernel(in_ref, _, out_ref):
    taps, _, f_part = out_ref.shape
    total = sum(in_ref[p].astype(jnp.float32) for p in range(in_ref.shape[0]))
    for tap in range(taps):
        out_ref[tap] = total[:, tap * f_part : (tap + 1) * f_part]


def finish(pieces, taps, f_part, after):
    return pl.pallas_call(
        finish_kernel,
        in_specs=[IN_VMEM, ANYWHERE],
        out_shape=struct((taps, pieces.shape[1], f_part), jnp.float32),
        compiler_params=params(8),
        cost_estimate=cost(0, 4 * pieces.size),
        name="finish",
    )(pieces, after)


def act_kernel(in_ref, _, *out_refs):
    for sample, out_ref in enumerate(out_refs):
        normed, _ = normalize(in_ref[sample])
        out_ref[...] = gelu_tanh(normed).astype(out_ref.dtype)


def activate(inputs, block, after):
    samples, bins, width = inputs.shape
    return pl.pallas_call(
        act_kernel,
        grid=(bins // block,),
        in_specs=[pl.BlockSpec((samples, block, width), lambda i: (0, i, 0)), ANYWHERE],
        out_specs=[pl.BlockSpec((block, width), lambda i: (i, 0))] * samples,
        out_shape=[struct((bins, width), inputs.dtype)] * samples,
        compiler_params=params(8),
        cost_estimate=cost(20 * inputs.size, 4 * inputs.size),
        name="activate",
    )(inputs, after)


def roles(yh):
    return (2 * yh, 1, 2 - 2 * yh)


def join_weights(sides, joined, point, yh, zl):
    for side, refs in enumerate(sides):
        for low, ref in enumerate(refs):
            pairs, far, span, lanes = ref.shape
            near, half = 2 * pairs, lanes // 4
            columns = slice(side * half, (side + 1) * half)
            for high in range(pairs):
                for zh in range(far):
                    first = (zh * near + (zl ^ (2 * high + low))) * span
                    rows = pl.ds(pl.multiple_of(first, span), span)
                    block = ref[high, zh]
                    for tap, role in enumerate(roles(yh)):
                        joined[role, rows, columns] = block[:, tap * half : (tap + 1) * half]
                    if point is not None:
                        point[rows, columns] = block[:, 3 * half :]


def forward_kernel(scale, samples, at_ref, *refs):
    count = 3 * samples + 1
    far_refs, refs = refs[: count + 4], refs[count + 4 :]
    pre_ref, own_out, other_out, acts, cot, packed, weights, point, turned, sems = refs
    _, bins, width = cot.shape
    half = weights.shape[2] // CORES
    near_refs = [acts.at[i] for i in range(3 * samples)] + [cot] + [packed.at[i] for i in range(4)]
    copies = [
        pltpu.make_async_copy(far_ref, near_ref, sems.at[i])
        for i, (far_ref, near_ref) in enumerate(zip(far_refs, near_refs))
    ]
    for copy in copies[count:]:
        copy.start()
    for sample in range(samples):
        for role in range(3):
            copies[role * samples + sample].start()
        if sample == 0:
            copies[count - 1].start()
    for copy in copies[count:]:
        copy.wait()
    sides = [[packed.at[2 * side + low] for low in range(2)] for side in range(CORES)]
    join_weights(sides, weights, point, at_ref[0], at_ref[1])
    for sample in range(samples):
        for role in range(3):
            copies[role * samples + sample].wait()
        if sample == 0:
            copies[count - 1].wait()
        handed, mid, partner = [acts[role * samples + sample] for role in range(3)]
        shifted = dot(handed, weights[0], 1, 0).astype(jnp.bfloat16).astype(jnp.float32)
        shifted += dot(partner, weights[2], 1, 0).astype(jnp.bfloat16).astype(jnp.float32)
        preact = shifted + dot(mid, weights[1], 1, 0)
        grad_inner = dot(cot[sample], point[...], 1, 0)
        grad_pre = grad_inner * gelu_slope(preact)
        pre_ref[sample] = grad_pre.astype(jnp.bfloat16)
        turned[sample] = grad_pre.T.astype(jnp.bfloat16)
    for role, tap in enumerate(roles(at_ref[0])):
        term = sum(
            dot(turned[sample], acts[role * samples + sample], 1, 0) for sample in range(samples)
        )
        term = term * scale
        own_out[:, tap] = term[:half].reshape(own_out.shape[0], -1, width)
        other = term[half:].astype(jnp.bfloat16)
        other_out[:, tap] = other.reshape(other_out.shape[0], -1, width)


def forward(at, acts, cotangent, own_w, other_w, scale):
    samples, bins, width = cotangent.shape
    hidden = CORES * own_w[0].shape[3] // 4
    half = (X_PARTS, 3, hidden // CORES // X_PARTS, width)
    count = 3 * samples
    return pl.pallas_call(
        functools.partial(forward_kernel, scale, samples),
        in_specs=[IN_SMEM] + [IN_HBM] * (count + 5),
        out_specs=[IN_VMEM] * 3,
        out_shape=[
            struct((samples, bins, hidden), jnp.bfloat16),
            struct(half, jnp.float32),
            struct(half, jnp.bfloat16),
        ],
        scratch_shapes=[
            pltpu.VMEM((count, bins, width), jnp.bfloat16),
            pltpu.VMEM(cotangent.shape, jnp.bfloat16),
            pltpu.VMEM((4,) + own_w[0].shape, jnp.bfloat16),
            pltpu.VMEM((3, width, hidden), jnp.bfloat16),
            pltpu.VMEM((width, hidden), jnp.bfloat16),
            pltpu.VMEM((samples, hidden, bins), jnp.bfloat16),
            pltpu.SemaphoreType.DMA((count + 5,)),
        ],
        compiler_params=params(30),
        cost_estimate=cost(14 * samples * bins * width * hidden, 16 * samples * bins * width),
        name="forward",
    )(at, *[in_hbm(array) for array in (*acts, cotangent)], *own_w, *other_w)


def backward_kernel(at_ref, in_ref, cot_ref, partner_ref, pre_ref, handed_ref, *refs):
    packed, (out_ref, token_ref, weights) = refs[:4], refs[4:]

    @pl.when(pl.program_id(0) == 0)
    def _():
        join_weights((packed[:2], packed[2:]), weights, None, at_ref[0], at_ref[1])
        token_ref[...] = jnp.zeros_like(token_ref)

    for sample in range(in_ref.shape[0]):
        grad_act = (
            dot(partner_ref[sample], weights[0], 1, 1)
            + dot(pre_ref[sample], weights[1], 1, 1)
            + dot(handed_ref[sample], weights[2], 1, 1)
        )
        normed, row_scale = normalize(in_ref[sample])
        grad_norm = grad_act * gelu_slope(normed)
        center = jnp.mean(grad_norm * normed, axis=-1, keepdims=True)
        grad = cot_ref[sample].astype(jnp.float32) + row_scale * (grad_norm - normed * center)
        out_ref[sample] = grad.astype(out_ref.dtype)


def backward(at, inputs, cotangent, partner, grad_pre, handed, packed, block):
    samples, bins, width = inputs.shape
    hidden = grad_pre.shape[2]
    wide = pl.BlockSpec((samples, block, width), lambda i: (0, i, 0))
    narrow = pl.BlockSpec((samples, block, hidden), lambda i: (0, i, 0))
    whole = pl.BlockSpec(
        packed[0].shape, lambda i: (0, 0, 0, 0), pipeline_mode=pl.Buffered(1)
    )
    return pl.pallas_call(
        backward_kernel,
        grid=(bins // block,),
        in_specs=[IN_SMEM, wide, wide, narrow, narrow, narrow] + [whole] * 4,
        out_specs=[wide, pl.BlockSpec((8, LANES), lambda i: (0, 0))],
        out_shape=[struct(inputs.shape, inputs.dtype), struct((8, LANES), jnp.float32)],
        scratch_shapes=[pltpu.VMEM((3, width, hidden), jnp.bfloat16)],
        compiler_params=params(24),
        cost_estimate=cost(6 * samples * bins * width * hidden, 16 * samples * bins * width),
        name="backward",
    )(
        at,
        in_hbm(inputs),
        in_hbm(cotangent),
        partner,
        grad_pre,
        handed,
        *packed,
    )


def exchanged(array):
    return lax.ppermute(array, "yh", [(0, 1), (1, 0)])


def handed_on(array):
    lower = [(Y_PARTS * i, Y_PARTS * (i + 1)) for i in range(X_PARTS - 1)]
    higher = [(Y_PARTS * (i + 1) + 1, Y_PARTS * i + 1) for i in range(X_PARTS - 1)]
    return lax.ppermute(array, ("x", "yh"), lower + higher)


def z_pair(array, bit):
    near = lax.axis_size("zl")
    return lax.ppermute(array, "zl", [(i, i ^ bit) for i in range(near)])


def other_core(array):
    return lax.ppermute(array, "core", [(0, 1), (1, 0)])


def body(inputs, conv_weight, point_weight, cotangent):
    samples, bins, width = inputs.shape
    taps, c_part, f_part = conv_weight.shape
    near, far = lax.axis_size("zl"), lax.axis_size("zh")
    depth = near * far
    blocks = X_PARTS * Y_PARTS
    devices = depth * Y_PARTS * blocks * CORES
    grad_scale = float(samples * bins * devices) ** (-0.5)
    at = jnp.stack([lax.axis_index("yh"), lax.axis_index("zl")]).astype(jnp.int32)

    packed = pack(conv_weight, point_weight, blocks * Y_PARTS)
    pieces = lax.all_to_all(packed, ("x", "yh", "yl"), 0, 0)

    mids = list(activate(inputs, 256, pieces))
    partners = [exchanged(mid) for mid in mids]

    part = lax.all_to_all(assemble(pieces, f_part, taps + 1)[:far], "zh", 0, 0)
    part = once(part, partners[0])
    handed = [handed_on(partners[0])]
    two = once(jnp.stack([part, z_pair(part, 2)]), handed[0], partners[1])
    handed.append(handed_on(partners[1]))
    other_two = other_core(two)
    last = once(z_pair(two, 1), handed[1])

    packed = (two, last, other_two, other_core(last))

    grad_pre, own, other = forward(
        at, handed + mids + partners, cotangent, packed[:2], packed[2:], grad_scale
    )

    def first_sums(own, other):
        pair = own + other_core(other).astype(jnp.float32)
        return lax.all_to_all(pair.astype(jnp.bfloat16), "x", 0, 0)

    def second_sums(part):
        return lax.all_to_all(part, ("zh", "zl"), 0, 0)

    grad_partner = exchanged(grad_pre)
    parts = held(first_sums, own, other)
    grad_handed = handed_on(once(grad_partner, parts))
    parts = held(second_sums, by_channel(parts, f_part, depth))
    sums = add_parts(parts.reshape(depth, Y_PARTS * Y_PARTS, c_part, LANES))
    pieces = lax.all_to_all(sums, ("yh", "yl"), 0, 0)

    input_grad, token = backward(
        at, inputs, cotangent, grad_partner, grad_pre, grad_handed, packed, 256
    )
    return (input_grad, finish(pieces, taps, f_part, token))


def solution(mesh):
    depth = mesh.shape["dp"] // Y_PARTS
    fine = Mesh(
        mesh.devices.reshape(depth // Z_PARTS, Z_PARTS, Y_PARTS, X_PARTS, Y_PARTS, CORES),
        ("zh", "zl", "yl", "x", "yh", "core"),
    )
    dp, seq = ("zh", "zl", "yl"), ("x", "yh", "core")
    return jax.shard_map(
        body,
        mesh=fine,
        in_specs=(P(dp, seq, None), P(None, dp, seq), P(seq, dp), P(dp, seq, None)),
        out_specs=(P(dp, seq, None), P(None, dp, seq)),
        check_vma=False,
    )
```

```python
import functools

import jax
import jax.numpy as jnp
from jax import lax
from jax.experimental import pallas as pl
from jax.experimental.pallas import tpu as pltpu
from jax.sharding import Mesh
from jax.sharding import PartitionSpec as P

LANES = 128
X_PARTS, Y_PARTS, Z_PARTS, CORES = 4, 2, 4, 2
MIB = 1024 * 1024

EPSILON = 1e-06
GELU_SCALE = 0.7978845608028654
GELU_CUBIC = 0.044715


def gelu_tanh(values):
    return (
        0.5
        * values
        * (1.0 + jnp.tanh(GELU_SCALE * (values + GELU_CUBIC * values * values * values)))
    )


def gelu_slope(values):
    tangent = jnp.tanh(GELU_SCALE * (values + GELU_CUBIC * values * values * values))
    return 0.5 * (1.0 + tangent) + 0.5 * values * (1.0 - tangent * tangent) * GELU_SCALE * (
        1.0 + 3.0 * GELU_CUBIC * values * values
    )


def dot(left, right, left_dim, right_dim):
    return lax.dot_general(
        left, right, (((left_dim,), (right_dim,)), ((), ())), preferred_element_type=jnp.float32
    )


def normalize(values):
    floats = values.astype(jnp.float32)
    row_scale = lax.rsqrt(jnp.mean(floats * floats, axis=-1, keepdims=True) + EPSILON)
    return floats * row_scale, row_scale


def params(mib):
    return pltpu.CompilerParams(vmem_limit_bytes=mib * MIB)


def struct(shape, dtype):
    return jax.ShapeDtypeStruct(shape, dtype)


def cost(flops, nbytes):
    return pl.CostEstimate(flops=flops, bytes_accessed=nbytes, transcendentals=0)


ANYWHERE = pl.BlockSpec(memory_space=pl.ANY)
IN_VMEM = pl.BlockSpec(memory_space=pltpu.VMEM)
IN_HBM = pl.BlockSpec(memory_space=pltpu.HBM)
IN_SMEM = pl.BlockSpec(memory_space=pltpu.SMEM)


def in_hbm(array):
    return pltpu.with_memory_space_constraint(array, pltpu.HBM)


def once_kernel(in_ref, *refs):
    refs[-1][...] = in_ref[...]


def once(array, *after):
    return pl.pallas_call(
        once_kernel,
        in_specs=[IN_VMEM] + [ANYWHERE] * len(after),
        out_shape=struct(array.shape, array.dtype),
        compiler_params=params(8),
        cost_estimate=cost(0, 4 * array.size),
        name="once",
    )(array, *after)


def held(stage, *args):
    def blank(*args):
        return jnp.zeros(out.shape, out.dtype)

    out = jax.eval_shape(stage, *args)
    return lax.cond(lax.axis_index("x") < X_PARTS, stage, blank, *args)


def pack_kernel(conv_ref, point_ref, out_ref):
    taps, c_part, f_part = conv_ref.shape
    pieces = [conv_ref[tap].astype(jnp.float32) for tap in range(taps)]
    pieces.append(point_ref[...].astype(jnp.float32).T)
    pieces.append(jnp.zeros((c_part, LANES - (taps + 1) * f_part), jnp.float32))
    packed = jnp.concatenate(pieces, axis=1).astype(out_ref.dtype)
    out_ref[...] = jnp.broadcast_to(packed[None], out_ref.shape)


def pack(conv_weight, point_weight, peers):
    c_part = conv_weight.shape[1]
    return pl.pallas_call(
        pack_kernel,
        out_shape=struct((peers, c_part, LANES), conv_weight.dtype),
        compiler_params=params(8),
        cost_estimate=cost(0, 2 * peers * c_part * LANES),
        name="pack",
    )(conv_weight, point_weight)


def assemble_kernel(f_part, taps, in_ref, out_ref):
    blocks = in_ref.shape[0] // Y_PARTS
    for low in range(Y_PARTS):
        pieces = [in_ref[Y_PARTS * block + low].astype(jnp.float32) for block in range(blocks)]
        rows = jnp.concatenate(
            [
                piece[:, tap * f_part : (tap + 1) * f_part]
                for tap in range(taps)
                for piece in pieces
            ],
            axis=1,
        )
        span = rows.shape[0]
        for copy in range(Z_PARTS):
            out_ref[copy, pl.ds(low * span, span), :] = rows.astype(out_ref.dtype)


def assemble(gathered, f_part, taps):
    peers, c_part, _ = gathered.shape
    lanes = peers // Y_PARTS * taps * f_part
    return pl.pallas_call(
        functools.partial(assemble_kernel, f_part, taps),
        out_shape=struct((Z_PARTS, Y_PARTS * c_part, lanes), gathered.dtype),
        compiler_params=params(8),
        cost_estimate=cost(0, 4 * gathered.size * 2),
        name="assemble",
    )(gathered)


def by_channel_kernel(in_ref, out_ref):
    peers, taps, rows, width = in_ref.shape
    depth, _, c_part, _ = out_ref.shape
    total = [sum(in_ref[p, tap].astype(jnp.float32) for p in range(peers)) for tap in range(taps)]
    turned = jnp.concatenate(total, axis=0).T.reshape(depth, Y_PARTS, c_part, taps * rows)
    blank = jnp.zeros((depth, c_part, LANES - Y_PARTS * rows), jnp.float32)
    for tap in range(taps):
        lanes = slice(tap * rows, (tap + 1) * rows)
        parts = [turned[:, low, :, lanes] for low in range(Y_PARTS)] + [blank]
        out_ref[:, tap] = jnp.concatenate(parts, axis=2).astype(out_ref.dtype)


def by_channel(parts, depth):
    taps, c_part = parts.shape[1], parts.shape[3] // (depth * Y_PARTS)
    return pl.pallas_call(
        by_channel_kernel,
        out_shape=struct((depth, taps, c_part, LANES), parts.dtype),
        compiler_params=params(16),
        cost_estimate=cost(0, 4 * parts.size),
        name="by_channel",
    )(parts)


def add_kernel(f_part, in_ref, _, out_ref):
    peers, taps, c_part, _ = in_ref.shape
    total = [sum(in_ref[p, tap].astype(jnp.float32) for p in range(peers)) for tap in range(taps)]
    blank = jnp.zeros((c_part, LANES - taps * f_part), jnp.float32)
    for low in range(Y_PARTS):
        for high in range(Y_PARTS):
            first = (low * Y_PARTS + high) * f_part
            parts = [t[:, first : first + f_part] for t in total] + [blank]
            out_ref[high * Y_PARTS + low] = jnp.concatenate(parts, axis=1).astype(out_ref.dtype)


def add_parts(parts, f_part, after):
    return pl.pallas_call(
        functools.partial(add_kernel, f_part),
        in_specs=[IN_VMEM, ANYWHERE],
        out_shape=struct((Y_PARTS * Y_PARTS,) + parts.shape[2:], parts.dtype),
        compiler_params=params(8),
        cost_estimate=cost(0, 4 * parts.size),
        name="add_parts",
    )(parts, after)


def finish_kernel(in_ref, out_ref):
    taps, _, f_part = out_ref.shape
    total = sum(in_ref[p].astype(jnp.float32) for p in range(in_ref.shape[0]))
    for tap in range(taps):
        out_ref[tap] = total[:, tap * f_part : (tap + 1) * f_part]


def finish(pieces, taps, f_part):
    return pl.pallas_call(
        finish_kernel,
        out_shape=struct((taps, pieces.shape[1], f_part), jnp.float32),
        compiler_params=params(8),
        cost_estimate=cost(0, 4 * pieces.size),
        name="finish",
    )(pieces)


def act_kernel(in_ref, _, *out_refs):
    for sample, out_ref in enumerate(out_refs):
        normed, _ = normalize(in_ref[sample])
        out_ref[...] = gelu_tanh(normed).astype(out_ref.dtype)


def activate(inputs, block, after):
    samples, bins, width = inputs.shape
    return pl.pallas_call(
        act_kernel,
        grid=(bins // block,),
        in_specs=[pl.BlockSpec((samples, block, width), lambda i: (0, i, 0)), ANYWHERE],
        out_specs=[pl.BlockSpec((block, width), lambda i: (i, 0))] * samples,
        out_shape=[struct((bins, width), inputs.dtype)] * samples,
        compiler_params=params(8),
        cost_estimate=cost(20 * inputs.size, 4 * inputs.size),
        name="activate",
    )(inputs, after)


def roles(yh):
    return (2 * yh, 1, 2 - 2 * yh)


def join_weights(sides, joined, point, yh, zl):
    for side, refs in enumerate(sides):
        for low, ref in enumerate(refs):
            pairs, far, span, lanes = ref.shape
            near, half = 2 * pairs, lanes // 4
            columns = slice(side * half, (side + 1) * half)
            for high in range(pairs):
                for zh in range(far):
                    first = (zh * near + (zl ^ (2 * high + low))) * span
                    rows = pl.ds(pl.multiple_of(first, span), span)
                    block = ref[high, zh]
                    for tap, role in enumerate(roles(yh)):
                        joined[role, rows, columns] = block[:, tap * half : (tap + 1) * half]
                    if point is not None:
                        point[rows, columns] = block[:, 3 * half :]


def forward_kernel(scale, samples, at_ref, *refs):
    count = 3 * samples + 1
    far_refs, refs = refs[: count + 4], refs[count + 4 :]
    pre_ref, own_out, other_out, acts, cot, packed, weights, point, turned, sems = refs
    _, bins, width = cot.shape
    half = weights.shape[2] // CORES
    near_refs = [acts.at[i] for i in range(3 * samples)] + [cot] + [packed.at[i] for i in range(4)]
    copies = [
        pltpu.make_async_copy(far_ref, near_ref, sems.at[i])
        for i, (far_ref, near_ref) in enumerate(zip(far_refs, near_refs))
    ]
    for copy in copies[count:]:
        copy.start()
    for sample in range(samples):
        for role in range(3):
            copies[role * samples + sample].start()
        if sample == 0:
            copies[count - 1].start()
    for copy in copies[count:]:
        copy.wait()
    sides = [[packed.at[2 * side + low] for low in range(2)] for side in range(CORES)]
    join_weights(sides, weights, point, at_ref[0], at_ref[1])
    for sample in range(samples):
        for role in range(3):
            copies[role * samples + sample].wait()
        if sample == 0:
            copies[count - 1].wait()
        handed, mid, partner = [acts[role * samples + sample] for role in range(3)]
        shifted = dot(handed, weights[0], 1, 0).astype(jnp.bfloat16).astype(jnp.float32)
        shifted += dot(partner, weights[2], 1, 0).astype(jnp.bfloat16).astype(jnp.float32)
        preact = shifted + dot(mid, weights[1], 1, 0)
        grad_inner = dot(cot[sample], point[...], 1, 0)
        grad_pre = grad_inner * gelu_slope(preact)
        pre_ref[sample] = grad_pre.astype(jnp.bfloat16)
        turned[sample] = grad_pre.T.astype(jnp.bfloat16)
    for role, tap in enumerate(roles(at_ref[0])):
        term = sum(
            dot(turned[sample], acts[role * samples + sample], 1, 0) for sample in range(samples)
        )
        term = term * scale
        own_out[:, tap] = term[:half].reshape(own_out.shape[0], -1, width)
        other = term[half:].astype(jnp.bfloat16)
        other_out[:, tap] = other.reshape(other_out.shape[0], -1, width)


def forward(at, acts, cotangent, own_w, other_w, scale):
    samples, bins, width = cotangent.shape
    hidden = CORES * own_w[0].shape[3] // 4
    half = (X_PARTS, 3, hidden // CORES // X_PARTS, width)
    count = 3 * samples
    return pl.pallas_call(
        functools.partial(forward_kernel, scale, samples),
        in_specs=[IN_SMEM] + [IN_HBM] * (count + 5),
        out_specs=[IN_VMEM] * 3,
        out_shape=[
            struct((samples, bins, hidden), jnp.bfloat16),
            struct(half, jnp.float32),
            struct(half, jnp.bfloat16),
        ],
        scratch_shapes=[
            pltpu.VMEM((count, bins, width), jnp.bfloat16),
            pltpu.VMEM(cotangent.shape, jnp.bfloat16),
            pltpu.VMEM((4,) + own_w[0].shape, jnp.bfloat16),
            pltpu.VMEM((3, width, hidden), jnp.bfloat16),
            pltpu.VMEM((width, hidden), jnp.bfloat16),
            pltpu.VMEM((samples, hidden, bins), jnp.bfloat16),
            pltpu.SemaphoreType.DMA((count + 5,)),
        ],
        compiler_params=params(30),
        cost_estimate=cost(14 * samples * bins * width * hidden, 16 * samples * bins * width),
        name="forward",
    )(at, *[in_hbm(array) for array in (*acts, cotangent)], *own_w, *other_w)


def backward_kernel(at_ref, in_ref, cot_ref, partner_ref, pre_ref, handed_ref, *refs):
    packed, (out_ref, token_ref, weights) = refs[:4], refs[4:]

    @pl.when(pl.program_id(0) == 0)
    def _():
        join_weights((packed[:2], packed[2:]), weights, None, at_ref[0], at_ref[1])
        token_ref[...] = jnp.zeros_like(token_ref)

    for sample in range(in_ref.shape[0]):
        grad_act = (
            dot(partner_ref[sample], weights[0], 1, 1)
            + dot(pre_ref[sample], weights[1], 1, 1)
            + dot(handed_ref[sample], weights[2], 1, 1)
        )
        normed, row_scale = normalize(in_ref[sample])
        grad_norm = grad_act * gelu_slope(normed)
        center = jnp.mean(grad_norm * normed, axis=-1, keepdims=True)
        grad = cot_ref[sample].astype(jnp.float32) + row_scale * (grad_norm - normed * center)
        out_ref[sample] = grad.astype(out_ref.dtype)


def backward(at, inputs, cotangent, partner, grad_pre, handed, packed, block):
    samples, bins, width = inputs.shape
    hidden = grad_pre.shape[2]
    wide = pl.BlockSpec((samples, block, width), lambda i: (0, i, 0))
    narrow = pl.BlockSpec((samples, block, hidden), lambda i: (0, i, 0))
    whole = pl.BlockSpec(
        packed[0].shape, lambda i: (0, 0, 0, 0), pipeline_mode=pl.Buffered(1)
    )
    return pl.pallas_call(
        backward_kernel,
        grid=(bins // block,),
        in_specs=[IN_SMEM, wide, wide, narrow, narrow, narrow] + [whole] * 4,
        out_specs=[wide, pl.BlockSpec((8, LANES), lambda i: (0, 0))],
        out_shape=[struct(inputs.shape, inputs.dtype), struct((8, LANES), jnp.float32)],
        scratch_shapes=[pltpu.VMEM((3, width, hidden), jnp.bfloat16)],
        compiler_params=params(24),
        cost_estimate=cost(6 * samples * bins * width * hidden, 16 * samples * bins * width),
        name="backward",
    )(
        at,
        in_hbm(inputs),
        in_hbm(cotangent),
        partner,
        grad_pre,
        handed,
        *packed,
    )


def exchanged(array):
    return lax.ppermute(array, "yh", [(0, 1), (1, 0)])


def handed_on(array):
    lower = [(Y_PARTS * i, Y_PARTS * (i + 1)) for i in range(X_PARTS - 1)]
    higher = [(Y_PARTS * (i + 1) + 1, Y_PARTS * i + 1) for i in range(X_PARTS - 1)]
    return lax.ppermute(array, ("x", "yh"), lower + higher)


def z_pair(array, bit):
    near = lax.axis_size("zl")
    return lax.ppermute(array, "zl", [(i, i ^ bit) for i in range(near)])


def other_core(array):
    return lax.ppermute(array, "core", [(0, 1), (1, 0)])


def body(inputs, conv_weight, point_weight, cotangent):
    samples, bins, width = inputs.shape
    taps, c_part, f_part = conv_weight.shape
    near, far = lax.axis_size("zl"), lax.axis_size("zh")
    depth = near * far
    blocks = X_PARTS * Y_PARTS
    devices = depth * Y_PARTS * blocks * CORES
    grad_scale = float(samples * bins * devices) ** (-0.5)
    at = jnp.stack([lax.axis_index("yh"), lax.axis_index("zl")]).astype(jnp.int32)

    packed = pack(conv_weight, point_weight, blocks * Y_PARTS)
    pieces = lax.all_to_all(packed, ("x", "yh", "yl"), 0, 0)

    mids = list(activate(inputs, 256, pieces))
    partners = [exchanged(mid) for mid in mids]

    part = lax.all_to_all(assemble(pieces, f_part, taps + 1)[:far], "zh", 0, 0)
    part = once(part, partners[0])
    handed = [handed_on(partners[0])]
    two = once(jnp.stack([part, z_pair(part, 2)]), handed[0], partners[1])
    handed.append(handed_on(partners[1]))
    other_two = other_core(two)
    last = once(z_pair(two, 1), handed[1])

    packed = (two, last, other_two, other_core(last))

    grad_pre, own, other = forward(
        at, handed + mids + partners, cotangent, packed[:2], packed[2:], grad_scale
    )

    def first_sums(own, other):
        pair = own + other_core(other).astype(jnp.float32)
        return lax.all_to_all(pair.astype(jnp.bfloat16), "x", 0, 0)

    grad_partner = exchanged(grad_pre)
    parts = held(first_sums, own, other)
    grad_handed = handed_on(once(grad_partner, parts))
    parts = lax.all_to_all(by_channel(parts, depth), ("zh", "zl"), 0, 0)
    input_grad, token = backward(
        at, inputs, cotangent, grad_partner, grad_pre, grad_handed, packed, 256
    )
    sums = add_parts(parts, f_part, token)
    conv_grad = finish(lax.all_to_all(sums, ("yh", "yl"), 0, 0), taps, f_part)
    return (input_grad, conv_grad)


def solution(mesh):
    depth = mesh.shape["dp"] // Y_PARTS
    fine = Mesh(
        mesh.devices.reshape(depth // Z_PARTS, Z_PARTS, Y_PARTS, X_PARTS, Y_PARTS, CORES),
        ("zh", "zl", "yl", "x", "yh", "core"),
    )
    dp, seq = ("zh", "zl", "yl"), ("x", "yh", "core")
    return jax.shard_map(
        body,
        mesh=fine,
        in_specs=(P(dp, seq, None), P(None, dp, seq), P(seq, dp), P(dp, seq, None)),
        out_specs=(P(dp, seq, None), P(None, dp, seq)),
        check_vma=False,
    )
```

```python
import functools

import jax
import jax.numpy as jnp
from jax import lax
from jax.experimental import pallas as pl
from jax.experimental.pallas import tpu as pltpu
from jax.sharding import Mesh
from jax.sharding import PartitionSpec as P

LANES = 128
X_PARTS, Y_PARTS, Z_PARTS, CORES = 4, 2, 4, 2
MIB = 1024 * 1024

EPSILON = 1e-06
GELU_SCALE = 0.7978845608028654
GELU_CUBIC = 0.044715


def gelu_tanh(values):
    return (
        0.5
        * values
        * (1.0 + jnp.tanh(GELU_SCALE * (values + GELU_CUBIC * values * values * values)))
    )


def gelu_slope(values):
    tangent = jnp.tanh(GELU_SCALE * (values + GELU_CUBIC * values * values * values))
    return 0.5 * (1.0 + tangent) + 0.5 * values * (1.0 - tangent * tangent) * GELU_SCALE * (
        1.0 + 3.0 * GELU_CUBIC * values * values
    )


def dot(left, right, left_dim, right_dim):
    return lax.dot_general(
        left, right, (((left_dim,), (right_dim,)), ((), ())), preferred_element_type=jnp.float32
    )


def normalize(values):
    floats = values.astype(jnp.float32)
    row_scale = lax.rsqrt(jnp.mean(floats * floats, axis=-1, keepdims=True) + EPSILON)
    return floats * row_scale, row_scale


def params(mib):
    return pltpu.CompilerParams(vmem_limit_bytes=mib * MIB)


def struct(shape, dtype):
    return jax.ShapeDtypeStruct(shape, dtype)


def cost(flops, nbytes):
    return pl.CostEstimate(flops=flops, bytes_accessed=nbytes, transcendentals=0)


ANYWHERE = pl.BlockSpec(memory_space=pl.ANY)
IN_VMEM = pl.BlockSpec(memory_space=pltpu.VMEM)
IN_HBM = pl.BlockSpec(memory_space=pltpu.HBM)
IN_SMEM = pl.BlockSpec(memory_space=pltpu.SMEM)


def in_hbm(array):
    return pltpu.with_memory_space_constraint(array, pltpu.HBM)


def once_kernel(in_ref, *refs):
    refs[-1][...] = in_ref[...]


def once(array, *after):
    return pl.pallas_call(
        once_kernel,
        in_specs=[IN_VMEM] + [ANYWHERE] * len(after),
        out_shape=struct(array.shape, array.dtype),
        compiler_params=params(8),
        cost_estimate=cost(0, 4 * array.size),
        name="once",
    )(array, *after)


def held(stage, *args):
    def blank(*args):
        return jnp.zeros(out.shape, out.dtype)

    out = jax.eval_shape(stage, *args)
    return lax.cond(lax.axis_index("x") < X_PARTS, stage, blank, *args)


def pack_kernel(conv_ref, point_ref, out_ref):
    taps, c_part, f_part = conv_ref.shape
    pieces = [conv_ref[tap].astype(jnp.float32) for tap in range(taps)]
    pieces.append(point_ref[...].astype(jnp.float32).T)
    pieces.append(jnp.zeros((c_part, LANES - (taps + 1) * f_part), jnp.float32))
    packed = jnp.concatenate(pieces, axis=1).astype(out_ref.dtype)
    out_ref[...] = jnp.broadcast_to(packed[None], out_ref.shape)


def pack(conv_weight, point_weight, peers):
    c_part = conv_weight.shape[1]
    return pl.pallas_call(
        pack_kernel,
        out_shape=struct((peers, c_part, LANES), conv_weight.dtype),
        compiler_params=params(8),
        cost_estimate=cost(0, 2 * peers * c_part * LANES),
        name="pack",
    )(conv_weight, point_weight)


def assemble_kernel(f_part, taps, in_ref, out_ref):
    blocks = in_ref.shape[0] // Y_PARTS
    for low in range(Y_PARTS):
        pieces = [in_ref[Y_PARTS * block + low].astype(jnp.float32) for block in range(blocks)]
        rows = jnp.concatenate(
            [
                piece[:, tap * f_part : (tap + 1) * f_part]
                for tap in range(taps)
                for piece in pieces
            ],
            axis=1,
        )
        span = rows.shape[0]
        for copy in range(Z_PARTS):
            out_ref[copy, pl.ds(low * span, span), :] = rows.astype(out_ref.dtype)


def assemble(gathered, f_part, taps):
    peers, c_part, _ = gathered.shape
    lanes = peers // Y_PARTS * taps * f_part
    return pl.pallas_call(
        functools.partial(assemble_kernel, f_part, taps),
        out_shape=struct((Z_PARTS, Y_PARTS * c_part, lanes), gathered.dtype),
        compiler_params=params(8),
        cost_estimate=cost(0, 4 * gathered.size * 2),
        name="assemble",
    )(gathered)


def by_channel_kernel(in_ref, out_ref):
    peers, taps, rows, width = in_ref.shape
    depth, _, c_part, _ = out_ref.shape
    total = [sum(in_ref[p, tap].astype(jnp.float32) for p in range(peers)) for tap in range(taps)]
    turned = jnp.concatenate(total, axis=0).T.reshape(depth, Y_PARTS, c_part, taps * rows)
    blank = jnp.zeros((depth, c_part, LANES - Y_PARTS * rows), jnp.float32)
    for tap in range(taps):
        lanes = slice(tap * rows, (tap + 1) * rows)
        parts = [turned[:, low, :, lanes] for low in range(Y_PARTS)] + [blank]
        out_ref[:, tap] = jnp.concatenate(parts, axis=2).astype(out_ref.dtype)


def by_channel(parts, depth):
    taps, c_part = parts.shape[1], parts.shape[3] // (depth * Y_PARTS)
    return pl.pallas_call(
        by_channel_kernel,
        out_shape=struct((depth, taps, c_part, LANES), parts.dtype),
        compiler_params=params(16),
        cost_estimate=cost(0, 4 * parts.size),
        name="by_channel",
    )(parts)


def add_kernel(f_part, in_ref, out_ref):
    peers, taps, c_part, _ = in_ref.shape
    total = [sum(in_ref[p, tap].astype(jnp.float32) for p in range(peers)) for tap in range(taps)]
    blank = jnp.zeros((c_part, LANES - taps * f_part), jnp.float32)
    for low in range(Y_PARTS):
        for high in range(Y_PARTS):
            first = (low * Y_PARTS + high) * f_part
            parts = [t[:, first : first + f_part] for t in total] + [blank]
            out_ref[high * Y_PARTS + low] = jnp.concatenate(parts, axis=1).astype(out_ref.dtype)


def add_parts(parts, f_part):
    return pl.pallas_call(
        functools.partial(add_kernel, f_part),
        out_shape=struct((Y_PARTS * Y_PARTS,) + parts.shape[2:], parts.dtype),
        compiler_params=params(8),
        cost_estimate=cost(0, 4 * parts.size),
        name="add_parts",
    )(parts)


def finish_kernel(in_ref, _, out_ref):
    taps, _, f_part = out_ref.shape
    total = sum(in_ref[p].astype(jnp.float32) for p in range(in_ref.shape[0]))
    for tap in range(taps):
        out_ref[tap] = total[:, tap * f_part : (tap + 1) * f_part]


def finish(pieces, taps, f_part, after):
    return pl.pallas_call(
        finish_kernel,
        in_specs=[IN_VMEM, ANYWHERE],
        out_shape=struct((taps, pieces.shape[1], f_part), jnp.float32),
        compiler_params=params(8),
        cost_estimate=cost(0, 4 * pieces.size),
        name="finish",
    )(pieces, after)


def act_kernel(in_ref, _, *out_refs):
    for sample, out_ref in enumerate(out_refs):
        normed, _ = normalize(in_ref[sample])
        out_ref[...] = gelu_tanh(normed).astype(out_ref.dtype)


def activate(inputs, block, after):
    samples, bins, width = inputs.shape
    return pl.pallas_call(
        act_kernel,
        grid=(bins // block,),
        in_specs=[pl.BlockSpec((samples, block, width), lambda i: (0, i, 0)), ANYWHERE],
        out_specs=[pl.BlockSpec((block, width), lambda i: (i, 0))] * samples,
        out_shape=[struct((bins, width), inputs.dtype)] * samples,
        compiler_params=params(8),
        cost_estimate=cost(20 * inputs.size, 4 * inputs.size),
        name="activate",
    )(inputs, after)


def roles(yh):
    return (2 * yh, 1, 2 - 2 * yh)


def join_weights(sides, joined, point, yh, zl):
    for side, refs in enumerate(sides):
        for low, ref in enumerate(refs):
            pairs, far, span, lanes = ref.shape
            near, half = 2 * pairs, lanes // 4
            columns = slice(side * half, (side + 1) * half)
            for high in range(pairs):
                for zh in range(far):
                    first = (zh * near + (zl ^ (2 * high + low))) * span
                    rows = pl.ds(pl.multiple_of(first, span), span)
                    block = ref[high, zh]
                    for tap, role in enumerate(roles(yh)):
                        joined[role, rows, columns] = block[:, tap * half : (tap + 1) * half]
                    if point is not None:
                        point[rows, columns] = block[:, 3 * half :]


def forward_kernel(scale, samples, at_ref, *refs):
    count = 3 * samples + 1
    far_refs, packed, refs = refs[:count], refs[count : count + 4], refs[count + 4 :]
    pre_ref, own_out, other_out, acts, cot, weights, point, turned, sems = refs
    _, bins, width = cot.shape
    half = weights.shape[2] // CORES
    near_refs = [acts.at[i] for i in range(3 * samples)] + [cot]
    copies = [
        pltpu.make_async_copy(far_ref, near_ref, sems.at[i])
        for i, (far_ref, near_ref) in enumerate(zip(far_refs, near_refs))
    ]
    for sample in range(samples):
        for role in range(3):
            copies[role * samples + sample].start()
        if sample == 0:
            copies[count - 1].start()
    join_weights((packed[:2], packed[2:]), weights, point, at_ref[0], at_ref[1])
    for sample in range(samples):
        for role in range(3):
            copies[role * samples + sample].wait()
        if sample == 0:
            copies[count - 1].wait()
        handed, mid, partner = [acts[role * samples + sample] for role in range(3)]
        shifted = dot(handed, weights[0], 1, 0).astype(jnp.bfloat16).astype(jnp.float32)
        shifted += dot(partner, weights[2], 1, 0).astype(jnp.bfloat16).astype(jnp.float32)
        preact = shifted + dot(mid, weights[1], 1, 0)
        grad_inner = dot(cot[sample], point[...], 1, 0)
        grad_pre = grad_inner * gelu_slope(preact)
        pre_ref[sample] = grad_pre.astype(jnp.bfloat16)
        turned[sample] = grad_pre.T.astype(jnp.bfloat16)
    for role, tap in enumerate(roles(at_ref[0])):
        term = sum(
            dot(turned[sample], acts[role * samples + sample], 1, 0) for sample in range(samples)
        )
        term = term * scale
        own_out[:, tap] = term[:half].reshape(own_out.shape[0], -1, width)
        other = term[half:].astype(jnp.bfloat16)
        other_out[:, tap] = other.reshape(other_out.shape[0], -1, width)


def forward(at, acts, cotangent, own_w, other_w, scale):
    samples, bins, width = cotangent.shape
    hidden = CORES * own_w[0].shape[3] // 4
    half = (X_PARTS, 3, hidden // CORES // X_PARTS, width)
    count = 3 * samples
    return pl.pallas_call(
        functools.partial(forward_kernel, scale, samples),
        in_specs=[IN_SMEM] + [IN_HBM] * (count + 1) + [IN_VMEM] * 4,
        out_specs=[IN_VMEM] * 3,
        out_shape=[
            struct((samples, bins, hidden), jnp.bfloat16),
            struct(half, jnp.float32),
            struct(half, jnp.bfloat16),
        ],
        scratch_shapes=[
            pltpu.VMEM((count, bins, width), jnp.bfloat16),
            pltpu.VMEM(cotangent.shape, jnp.bfloat16),
            pltpu.VMEM((3, width, hidden), jnp.bfloat16),
            pltpu.VMEM((width, hidden), jnp.bfloat16),
            pltpu.VMEM((samples, hidden, bins), jnp.bfloat16),
            pltpu.SemaphoreType.DMA((count + 1,)),
        ],
        compiler_params=params(30),
        cost_estimate=cost(14 * samples * bins * width * hidden, 16 * samples * bins * width),
        name="forward",
    )(at, *[in_hbm(array) for array in (*acts, cotangent)], *own_w, *other_w)


def backward_kernel(at_ref, in_ref, cot_ref, partner_ref, pre_ref, handed_ref, *refs):
    packed, (out_ref, token_ref, weights) = refs[:4], refs[4:]

    @pl.when(pl.program_id(0) == 0)
    def _():
        join_weights((packed[:2], packed[2:]), weights, None, at_ref[0], at_ref[1])
        token_ref[...] = jnp.zeros_like(token_ref)

    for sample in range(in_ref.shape[0]):
        grad_act = (
            dot(partner_ref[sample], weights[0], 1, 1)
            + dot(pre_ref[sample], weights[1], 1, 1)
            + dot(handed_ref[sample], weights[2], 1, 1)
        )
        normed, row_scale = normalize(in_ref[sample])
        grad_norm = grad_act * gelu_slope(normed)
        center = jnp.mean(grad_norm * normed, axis=-1, keepdims=True)
        grad = cot_ref[sample].astype(jnp.float32) + row_scale * (grad_norm - normed * center)
        out_ref[sample] = grad.astype(out_ref.dtype)


def backward(at, inputs, cotangent, partner, grad_pre, handed, packed, block):
    samples, bins, width = inputs.shape
    hidden = grad_pre.shape[2]
    wide = pl.BlockSpec((samples, block, width), lambda i: (0, i, 0))
    narrow = pl.BlockSpec((samples, block, hidden), lambda i: (0, i, 0))
    whole = pl.BlockSpec(
        packed[0].shape, lambda i: (0, 0, 0, 0), pipeline_mode=pl.Buffered(1)
    )
    return pl.pallas_call(
        backward_kernel,
        grid=(bins // block,),
        in_specs=[IN_SMEM, wide, wide, narrow, narrow, narrow] + [whole] * 4,
        out_specs=[wide, pl.BlockSpec((8, LANES), lambda i: (0, 0))],
        out_shape=[struct(inputs.shape, inputs.dtype), struct((8, LANES), jnp.float32)],
        scratch_shapes=[pltpu.VMEM((3, width, hidden), jnp.bfloat16)],
        compiler_params=params(24),
        cost_estimate=cost(6 * samples * bins * width * hidden, 16 * samples * bins * width),
        name="backward",
    )(
        at,
        in_hbm(inputs),
        in_hbm(cotangent),
        partner,
        grad_pre,
        handed,
        *[in_hbm(part) for part in packed],
    )


def exchanged(array):
    return lax.ppermute(array, "yh", [(0, 1), (1, 0)])


def handed_on(array):
    lower = [(Y_PARTS * i, Y_PARTS * (i + 1)) for i in range(X_PARTS - 1)]
    higher = [(Y_PARTS * (i + 1) + 1, Y_PARTS * i + 1) for i in range(X_PARTS - 1)]
    return lax.ppermute(array, ("x", "yh"), lower + higher)


def z_pair(array, bit):
    near = lax.axis_size("zl")
    return lax.ppermute(array, "zl", [(i, i ^ bit) for i in range(near)])


def other_core(array):
    return lax.ppermute(array, "core", [(0, 1), (1, 0)])


def body(inputs, conv_weight, point_weight, cotangent):
    samples, bins, width = inputs.shape
    taps, c_part, f_part = conv_weight.shape
    near, far = lax.axis_size("zl"), lax.axis_size("zh")
    depth = near * far
    blocks = X_PARTS * Y_PARTS
    devices = depth * Y_PARTS * blocks * CORES
    grad_scale = float(samples * bins * devices) ** (-0.5)
    at = jnp.stack([lax.axis_index("yh"), lax.axis_index("zl")]).astype(jnp.int32)

    packed = pack(in_hbm(conv_weight), in_hbm(point_weight), blocks * Y_PARTS)
    pieces = lax.all_to_all(packed, ("x", "yh", "yl"), 0, 0)

    mids = list(activate(in_hbm(inputs), 128, pieces))
    partners = [exchanged(mid) for mid in mids]

    part = lax.all_to_all(assemble(pieces, f_part, taps + 1)[:far], "zh", 0, 0)
    part = once(part, partners[0])
    handed = [handed_on(partners[0])]
    two = once(jnp.stack([part, z_pair(part, 2)]), handed[0], partners[1])
    handed.append(handed_on(partners[1]))
    other_two = other_core(two)
    last = once(z_pair(two, 1), handed[1])

    packed = (two, last, other_two, other_core(last))

    grad_pre, own, other = forward(
        at, handed + mids + partners, cotangent, packed[:2], packed[2:], grad_scale
    )

    def first_sums(own, other):
        pair = own + other.astype(jnp.float32)
        return lax.all_to_all(pair.astype(jnp.bfloat16), "x", 0, 0)

    other = other_core(other)
    grad_partner = exchanged(grad_pre)
    parts = held(first_sums, own, other)
    grad_handed = handed_on(once(grad_partner, parts))

    parts = lax.all_to_all(by_channel(parts, depth), ("zh", "zl"), 0, 0)
    input_grad, token = backward(
        at, inputs, cotangent, grad_partner, grad_pre, grad_handed, packed, 256
    )
    sums = add_parts(parts, f_part)
    conv_grad = finish(lax.all_to_all(sums, ("yh", "yl"), 0, 0), taps, f_part, token)
    return (input_grad, conv_grad)


def solution(mesh):
    depth = mesh.shape["dp"] // Y_PARTS
    fine = Mesh(
        mesh.devices.reshape(depth // Z_PARTS, Z_PARTS, Y_PARTS, X_PARTS, Y_PARTS, CORES),
        ("zh", "zl", "yl", "x", "yh", "core"),
    )
    dp, seq = ("zh", "zl", "yl"), ("x", "yh", "core")
    return jax.shard_map(
        body,
        mesh=fine,
        in_specs=(P(dp, seq, None), P(None, dp, seq), P(seq, dp), P(dp, seq, None)),
        out_specs=(P(dp, seq, None), P(None, dp, seq)),
        check_vma=False,
    )
```

```python
import functools

import jax
import jax.numpy as jnp
from jax import lax
from jax.experimental import pallas as pl
from jax.experimental.pallas import tpu as pltpu
from jax.sharding import Mesh
from jax.sharding import PartitionSpec as P

LANES = 128
SUBLANES = 8
X_PARTS, Y_PARTS, Z_PARTS, CORES = 4, 2, 4, 2
MIB = 1024 * 1024

EPSILON = 1e-06
GELU_SCALE = 0.7978845608028654
GELU_CUBIC = 0.044715


def gelu_tanh(values):
    return (
        0.5
        * values
        * (1.0 + jnp.tanh(GELU_SCALE * (values + GELU_CUBIC * values * values * values)))
    )


def gelu_slope(values):
    tangent = jnp.tanh(GELU_SCALE * (values + GELU_CUBIC * values * values * values))
    return 0.5 * (1.0 + tangent) + 0.5 * values * (1.0 - tangent * tangent) * GELU_SCALE * (
        1.0 + 3.0 * GELU_CUBIC * values * values
    )


def dot(left, right, left_dim, right_dim):
    return lax.dot_general(
        left, right, (((left_dim,), (right_dim,)), ((), ())), preferred_element_type=jnp.float32
    )


def normalize(values):
    floats = values.astype(jnp.float32)
    row_scale = lax.rsqrt(jnp.mean(floats * floats, axis=-1, keepdims=True) + EPSILON)
    return floats * row_scale, row_scale


def params(mib):
    return pltpu.CompilerParams(vmem_limit_bytes=mib * MIB)


def struct(shape, dtype):
    return jax.ShapeDtypeStruct(shape, dtype)


def cost(flops, nbytes):
    return pl.CostEstimate(flops=flops, bytes_accessed=nbytes, transcendentals=0)


ANYWHERE = pl.BlockSpec(memory_space=pl.ANY)
IN_VMEM = pl.BlockSpec(memory_space=pltpu.VMEM)
IN_HBM = pl.BlockSpec(memory_space=pltpu.HBM)
IN_SMEM = pl.BlockSpec(memory_space=pltpu.SMEM)


def in_hbm(array):
    return pltpu.with_memory_space_constraint(array, pltpu.HBM)


def once_kernel(in_ref, *refs):
    refs[-1][...] = in_ref[...]


def once(array, *after):
    return pl.pallas_call(
        once_kernel,
        in_specs=[IN_VMEM] + [ANYWHERE] * len(after),
        out_shape=struct(array.shape, array.dtype),
        compiler_params=params(8),
        cost_estimate=cost(0, 4 * array.size),
        name="once",
    )(array, *after)


def corner(array):
    return array[: 2 * SUBLANES, :LANES]


def held(stage, *args):
    def blank(*args):
        return jnp.zeros(out.shape, out.dtype)

    out = jax.eval_shape(stage, *args)
    return lax.cond(lax.axis_index("x") < X_PARTS, stage, blank, *args)


def pack_kernel(conv_ref, point_ref, out_ref):
    taps, c_part, f_part = conv_ref.shape
    pieces = [conv_ref[tap].astype(jnp.float32) for tap in range(taps)]
    pieces.append(point_ref[...].astype(jnp.float32).T)
    pieces.append(jnp.zeros((c_part, LANES - (taps + 1) * f_part), jnp.float32))
    packed = jnp.concatenate(pieces, axis=1).astype(out_ref.dtype)
    out_ref[...] = jnp.broadcast_to(packed[None], out_ref.shape)


def pack(conv_weight, point_weight, peers):
    c_part = conv_weight.shape[1]
    return pl.pallas_call(
        pack_kernel,
        out_shape=struct((peers, c_part, LANES), conv_weight.dtype),
        compiler_params=params(8),
        cost_estimate=cost(0, 2 * peers * c_part * LANES),
        name="pack",
    )(conv_weight, point_weight)


def assemble_kernel(f_part, taps, in_ref, out_ref):
    blocks = in_ref.shape[0] // Y_PARTS
    for low in range(Y_PARTS):
        pieces = [in_ref[Y_PARTS * block + low].astype(jnp.float32) for block in range(blocks)]
        rows = jnp.concatenate(
            [
                piece[:, tap * f_part : (tap + 1) * f_part]
                for tap in range(taps)
                for piece in pieces
            ],
            axis=1,
        )
        span = rows.shape[0]
        for copy in range(Z_PARTS):
            out_ref[copy, pl.ds(low * span, span), :] = rows.astype(out_ref.dtype)


def assemble(gathered, f_part, taps):
    peers, c_part, _ = gathered.shape
    lanes = peers // Y_PARTS * taps * f_part
    return pl.pallas_call(
        functools.partial(assemble_kernel, f_part, taps),
        out_shape=struct((Z_PARTS, Y_PARTS * c_part, lanes), gathered.dtype),
        compiler_params=params(8),
        cost_estimate=cost(0, 4 * gathered.size * 2),
        name="assemble",
    )(gathered)


def by_channel_kernel(in_ref, out_ref):
    peers, taps, rows, width = in_ref.shape
    depth, _, c_part, _ = out_ref.shape
    total = [sum(in_ref[p, tap].astype(jnp.float32) for p in range(peers)) for tap in range(taps)]
    turned = jnp.concatenate(total, axis=0).T.reshape(depth, Y_PARTS, c_part, taps * rows)
    blank = jnp.zeros((depth, c_part, LANES - Y_PARTS * rows), jnp.float32)
    for tap in range(taps):
        lanes = slice(tap * rows, (tap + 1) * rows)
        parts = [turned[:, low, :, lanes] for low in range(Y_PARTS)] + [blank]
        out_ref[:, tap] = jnp.concatenate(parts, axis=2).astype(out_ref.dtype)


def by_channel(parts, depth):
    taps, c_part = parts.shape[1], parts.shape[3] // (depth * Y_PARTS)
    return pl.pallas_call(
        by_channel_kernel,
        out_shape=struct((depth, taps, c_part, LANES), parts.dtype),
        compiler_params=params(16),
        cost_estimate=cost(0, 4 * parts.size),
        name="by_channel",
    )(parts)


def add_kernel(f_part, in_ref, out_ref):
    peers, taps, c_part, _ = in_ref.shape
    total = [sum(in_ref[p, tap].astype(jnp.float32) for p in range(peers)) for tap in range(taps)]
    blank = jnp.zeros((c_part, LANES - taps * f_part), jnp.float32)
    for low in range(Y_PARTS):
        for high in range(Y_PARTS):
            first = (low * Y_PARTS + high) * f_part
            parts = [t[:, first : first + f_part] for t in total] + [blank]
            out_ref[high * Y_PARTS + low] = jnp.concatenate(parts, axis=1).astype(out_ref.dtype)


def add_parts(parts, f_part):
    return pl.pallas_call(
        functools.partial(add_kernel, f_part),
        out_shape=struct((Y_PARTS * Y_PARTS,) + parts.shape[2:], parts.dtype),
        compiler_params=params(8),
        cost_estimate=cost(0, 4 * parts.size),
        name="add_parts",
    )(parts)


def finish_kernel(in_ref, _, out_ref):
    taps, _, f_part = out_ref.shape
    total = sum(in_ref[p].astype(jnp.float32) for p in range(in_ref.shape[0]))
    for tap in range(taps):
        out_ref[tap] = total[:, tap * f_part : (tap + 1) * f_part]


def finish(pieces, taps, f_part, after):
    return pl.pallas_call(
        finish_kernel,
        in_specs=[IN_VMEM, ANYWHERE],
        out_shape=struct((taps, pieces.shape[1], f_part), jnp.float32),
        compiler_params=params(8),
        cost_estimate=cost(0, 4 * pieces.size),
        name="finish",
    )(pieces, after)


def act_kernel(in_ref, _, *out_refs):
    for sample, out_ref in enumerate(out_refs):
        normed, _ = normalize(in_ref[sample])
        out_ref[...] = gelu_tanh(normed).astype(out_ref.dtype)


def activate(inputs, block, after):
    samples, bins, width = inputs.shape
    return pl.pallas_call(
        act_kernel,
        grid=(bins // block,),
        in_specs=[pl.BlockSpec((samples, block, width), lambda i: (0, i, 0)), ANYWHERE],
        out_specs=[pl.BlockSpec((block, width), lambda i: (i, 0))] * samples,
        out_shape=[struct((bins, width), inputs.dtype)] * samples,
        compiler_params=params(8),
        cost_estimate=cost(20 * inputs.size, 4 * inputs.size),
        name="activate",
    )(inputs, after)


def roles(yh):
    return (2 * yh, 1, 2 - 2 * yh)


def join_weights(sides, joined, point, yh, zl):
    for side, refs in enumerate(sides):
        for low, ref in enumerate(refs):
            pairs, far, span, lanes = ref.shape
            near, half = 2 * pairs, lanes // 4
            columns = slice(side * half, (side + 1) * half)
            for high in range(pairs):
                for zh in range(far):
                    first = (zh * near + (zl ^ (2 * high + low))) * span
                    rows = pl.ds(pl.multiple_of(first, span), span)
                    block = ref[high, zh]
                    for tap, role in enumerate(roles(yh)):
                        joined[role, rows, columns] = block[:, tap * half : (tap + 1) * half]
                    point[rows, columns] = block[:, 3 * half :]


def forward_kernel(scale, samples, at_ref, *refs):
    count = 3 * samples + 1
    far_refs, packed, refs = refs[:count], refs[count : count + 4], refs[count + 4 :]
    pre_ref, own_out, other_out, weights_out, acts, cot, weights, point, turned, sems = refs
    _, bins, width = cot.shape
    half = weights.shape[2] // CORES
    near_refs = [acts.at[i] for i in range(3 * samples)] + [cot]
    copies = [
        pltpu.make_async_copy(far_ref, near_ref, sems.at[i])
        for i, (far_ref, near_ref) in enumerate(zip(far_refs, near_refs))
    ]
    for sample in range(samples):
        for role in range(3):
            copies[role * samples + sample].start()
        if sample == 0:
            copies[count - 1].start()
    join_weights((packed[:2], packed[2:]), weights, point, at_ref[0], at_ref[1])
    keep = pltpu.make_async_copy(weights, weights_out, sems.at[count])
    keep.start()
    for sample in range(samples):
        for role in range(3):
            copies[role * samples + sample].wait()
        if sample == 0:
            copies[count - 1].wait()
        handed, mid, partner = [acts[role * samples + sample] for role in range(3)]
        shifted = dot(handed, weights[0], 1, 0).astype(jnp.bfloat16).astype(jnp.float32)
        shifted += dot(partner, weights[2], 1, 0).astype(jnp.bfloat16).astype(jnp.float32)
        preact = shifted + dot(mid, weights[1], 1, 0)
        grad_inner = dot(cot[sample], point[...], 1, 0)
        grad_pre = grad_inner * gelu_slope(preact)
        pre_ref[sample] = grad_pre.astype(jnp.bfloat16)
        turned[:, pl.ds(sample * bins, bins)] = grad_pre.T.astype(jnp.bfloat16)
    for role, tap in enumerate(roles(at_ref[0])):
        block = acts[pl.ds(role * samples, samples)].reshape(samples * bins, width)
        term = dot(turned[...], block, 1, 0) * scale
        own_out[:, tap] = term[:half].reshape(own_out.shape[0], -1, width)
        other = term[half:].astype(jnp.bfloat16)
        other_out[:, tap] = other.reshape(other_out.shape[0], -1, width)
    keep.wait()


def forward(at, acts, cotangent, own_w, other_w, scale):
    samples, bins, width = cotangent.shape
    hidden = CORES * own_w[0].shape[3] // 4
    half = (X_PARTS, 3, hidden // CORES // X_PARTS, width)
    count = 3 * samples
    return pl.pallas_call(
        functools.partial(forward_kernel, scale, samples),
        in_specs=[IN_SMEM] + [IN_HBM] * (count + 1) + [IN_VMEM] * 4,
        out_specs=[IN_VMEM] * 3 + [IN_HBM],
        out_shape=[
            struct((samples, bins, hidden), jnp.bfloat16),
            struct(half, jnp.float32),
            struct(half, jnp.bfloat16),
            struct((3, width, hidden), jnp.bfloat16),
        ],
        scratch_shapes=[
            pltpu.VMEM((count, bins, width), jnp.bfloat16),
            pltpu.VMEM(cotangent.shape, jnp.bfloat16),
            pltpu.VMEM((3, width, hidden), jnp.bfloat16),
            pltpu.VMEM((width, hidden), jnp.bfloat16),
            pltpu.VMEM((hidden, samples * bins), jnp.bfloat16),
            pltpu.SemaphoreType.DMA((count + 2,)),
        ],
        compiler_params=params(30),
        cost_estimate=cost(14 * samples * bins * width * hidden, 16 * samples * bins * width),
        name="forward",
    )(at, *[in_hbm(array) for array in (*acts, cotangent)], *own_w, *other_w)


def backward_kernel(in_ref, cot_ref, partner_ref, pre_ref, handed_ref, weights, out_ref, token_ref):
    token_ref[...] = jnp.zeros_like(token_ref)
    for sample in range(in_ref.shape[0]):
        grad_act = (
            dot(partner_ref[sample], weights[0], 1, 1)
            + dot(pre_ref[sample], weights[1], 1, 1)
            + dot(handed_ref[sample], weights[2], 1, 1)
        )
        normed, row_scale = normalize(in_ref[sample])
        grad_norm = grad_act * gelu_slope(normed)
        center = jnp.mean(grad_norm * normed, axis=-1, keepdims=True)
        grad = cot_ref[sample].astype(jnp.float32) + row_scale * (grad_norm - normed * center)
        out_ref[sample] = grad.astype(out_ref.dtype)


def backward(inputs, cotangent, partner, grad_pre, handed, weights, block):
    samples, bins, width = inputs.shape
    hidden = grad_pre.shape[2]
    wide = pl.BlockSpec((samples, block, width), lambda i: (0, i, 0))
    narrow = pl.BlockSpec((samples, block, hidden), lambda i: (0, i, 0))
    whole = pl.BlockSpec(weights.shape, lambda i: (0, 0, 0), pipeline_mode=pl.Buffered(1))
    return pl.pallas_call(
        backward_kernel,
        grid=(bins // block,),
        in_specs=[wide, wide, narrow, narrow, narrow, whole],
        out_specs=[wide, pl.BlockSpec((8, LANES), lambda i: (0, 0))],
        out_shape=[struct(inputs.shape, inputs.dtype), struct((8, LANES), jnp.float32)],
        compiler_params=params(24),
        cost_estimate=cost(6 * samples * bins * width * hidden, 16 * samples * bins * width),
        name="backward",
    )(in_hbm(inputs), in_hbm(cotangent), partner, grad_pre, handed, in_hbm(weights))


def exchanged(array):
    return lax.ppermute(array, "yh", [(0, 1), (1, 0)])


def handed_on(array):
    lower = [(Y_PARTS * i, Y_PARTS * (i + 1)) for i in range(X_PARTS - 1)]
    higher = [(Y_PARTS * (i + 1) + 1, Y_PARTS * i + 1) for i in range(X_PARTS - 1)]
    return lax.ppermute(array, ("x", "yh"), lower + higher)


def z_pair(array, bit):
    near = lax.axis_size("zl")
    return lax.ppermute(array, "zl", [(i, i ^ bit) for i in range(near)])


def other_core(array):
    return lax.ppermute(array, "core", [(0, 1), (1, 0)])


def body(inputs, conv_weight, point_weight, cotangent):
    samples, bins, width = inputs.shape
    taps, c_part, f_part = conv_weight.shape
    near, far = lax.axis_size("zl"), lax.axis_size("zh")
    depth = near * far
    blocks = X_PARTS * Y_PARTS
    devices = depth * Y_PARTS * blocks * CORES
    grad_scale = float(samples * bins * devices) ** (-0.5)
    at = jnp.stack([lax.axis_index("yh"), lax.axis_index("zl")]).astype(jnp.int32)

    packed = pack(in_hbm(conv_weight), in_hbm(point_weight), blocks * Y_PARTS)
    pieces = lax.all_to_all(packed, ("x", "yh", "yl"), 0, 0)

    mids = list(activate(in_hbm(inputs), 256, pieces))
    partners = [exchanged(mid) for mid in mids]

    part = lax.all_to_all(assemble(pieces, f_part, taps + 1)[:far], "zh", 0, 0)
    part = once(part, partners[0])
    handed = [handed_on(partners[0])]
    two = once(jnp.stack([part, z_pair(part, 2)]), corner(handed[0]), partners[1])
    handed.append(handed_on(partners[1]))
    other_two = other_core(two)
    last = once(z_pair(two, 1), corner(handed[1]))

    packed = (two, last, other_two, in_hbm(other_core(last)))

    grad_pre, own, other, weights = forward(
        at, handed + mids + partners, cotangent, packed[:2], packed[2:], grad_scale
    )

    def first_sums(own, other):
        pair = own + other.astype(jnp.float32)
        return lax.all_to_all(pair.astype(jnp.bfloat16), "x", 0, 0)

    other = other_core(other)
    grad_partner = exchanged(grad_pre)
    parts = held(first_sums, own, other)
    grad_handed = handed_on(once(grad_partner, parts))

    parts = lax.all_to_all(by_channel(parts, depth), ("zh", "zl"), 0, 0)
    input_grad, token = backward(
        inputs, cotangent, grad_partner, grad_pre, grad_handed, weights, 256
    )
    sums = add_parts(parts, f_part)
    conv_grad = finish(lax.all_to_all(sums, ("yh", "yl"), 0, 0), taps, f_part, token)
    return (input_grad, conv_grad)


def solution(mesh):
    depth = mesh.shape["dp"] // Y_PARTS
    fine = Mesh(
        mesh.devices.reshape(depth // Z_PARTS, Z_PARTS, Y_PARTS, X_PARTS, Y_PARTS, CORES),
        ("zh", "zl", "yl", "x", "yh", "core"),
    )
    dp, seq = ("zh", "zl", "yl"), ("x", "yh", "core")
    return jax.shard_map(
        body,
        mesh=fine,
        in_specs=(P(dp, seq, None), P(None, dp, seq), P(seq, dp), P(dp, seq, None)),
        out_specs=(P(dp, seq, None), P(None, dp, seq)),
        check_vma=False,
    )
```

```python
import functools

import jax
import jax.numpy as jnp
from jax import lax
from jax.experimental import pallas as pl
from jax.experimental.pallas import tpu as pltpu
from jax.sharding import Mesh
from jax.sharding import PartitionSpec as P

LANES = 128
SUBLANES = 8
X_PARTS, Y_PARTS, Z_PARTS, CORES = 4, 2, 4, 2
MIB = 1024 * 1024

EPSILON = 1e-06
GELU_SCALE = 0.7978845608028654
GELU_CUBIC = 0.044715


def gelu_tanh(values):
    return (
        0.5
        * values
        * (1.0 + jnp.tanh(GELU_SCALE * (values + GELU_CUBIC * values * values * values)))
    )


def gelu_slope(values):
    tangent = jnp.tanh(GELU_SCALE * (values + GELU_CUBIC * values * values * values))
    return 0.5 * (1.0 + tangent) + 0.5 * values * (1.0 - tangent * tangent) * GELU_SCALE * (
        1.0 + 3.0 * GELU_CUBIC * values * values
    )


def dot(left, right, left_dim, right_dim):
    return lax.dot_general(
        left, right, (((left_dim,), (right_dim,)), ((), ())), preferred_element_type=jnp.float32
    )


def normalize(values):
    floats = values.astype(jnp.float32)
    row_scale = lax.rsqrt(jnp.mean(floats * floats, axis=-1, keepdims=True) + EPSILON)
    return floats * row_scale, row_scale


def params(mib):
    return pltpu.CompilerParams(vmem_limit_bytes=mib * MIB)


def struct(shape, dtype):
    return jax.ShapeDtypeStruct(shape, dtype)


def cost(flops, nbytes):
    return pl.CostEstimate(flops=flops, bytes_accessed=nbytes, transcendentals=0)


ANYWHERE = pl.BlockSpec(memory_space=pl.ANY)
IN_VMEM = pl.BlockSpec(memory_space=pltpu.VMEM)
IN_HBM = pl.BlockSpec(memory_space=pltpu.HBM)
IN_SMEM = pl.BlockSpec(memory_space=pltpu.SMEM)


def in_hbm(array):
    return pltpu.with_memory_space_constraint(array, pltpu.HBM)


def once_kernel(in_ref, *refs):
    refs[-1][...] = in_ref[...]


def once(array, *after):
    return pl.pallas_call(
        once_kernel,
        in_specs=[IN_VMEM] + [ANYWHERE] * len(after),
        out_shape=struct(array.shape, array.dtype),
        compiler_params=params(8),
        cost_estimate=cost(0, 4 * array.size),
        name="once",
    )(array, *after)


def corner(array):
    return array[: 2 * SUBLANES, :LANES]


def held(stage, *args):
    def blank(*args):
        return jnp.zeros(out.shape, out.dtype)

    out = jax.eval_shape(stage, *args)
    return lax.cond(lax.axis_index("x") < X_PARTS, stage, blank, *args)


def pack_kernel(conv_ref, point_ref, out_ref):
    taps, c_part, f_part = conv_ref.shape
    pieces = [conv_ref[tap].astype(jnp.float32) for tap in range(taps)]
    pieces.append(point_ref[...].astype(jnp.float32).T)
    pieces.append(jnp.zeros((c_part, LANES - (taps + 1) * f_part), jnp.float32))
    packed = jnp.concatenate(pieces, axis=1).astype(out_ref.dtype)
    out_ref[...] = jnp.broadcast_to(packed[None], out_ref.shape)


def pack(conv_weight, point_weight, peers):
    c_part = conv_weight.shape[1]
    return pl.pallas_call(
        pack_kernel,
        out_shape=struct((peers, c_part, LANES), conv_weight.dtype),
        compiler_params=params(8),
        cost_estimate=cost(0, 2 * peers * c_part * LANES),
        name="pack",
    )(conv_weight, point_weight)


def assemble_kernel(f_part, taps, in_ref, out_ref):
    blocks = in_ref.shape[0] // Y_PARTS
    for low in range(Y_PARTS):
        pieces = [in_ref[Y_PARTS * block + low].astype(jnp.float32) for block in range(blocks)]
        rows = jnp.concatenate(
            [
                piece[:, tap * f_part : (tap + 1) * f_part]
                for tap in range(taps)
                for piece in pieces
            ],
            axis=1,
        )
        span = rows.shape[0]
        for copy in range(Z_PARTS):
            out_ref[copy, pl.ds(low * span, span), :] = rows.astype(out_ref.dtype)


def assemble(gathered, f_part, taps):
    peers, c_part, _ = gathered.shape
    lanes = peers // Y_PARTS * taps * f_part
    return pl.pallas_call(
        functools.partial(assemble_kernel, f_part, taps),
        out_shape=struct((Z_PARTS, Y_PARTS * c_part, lanes), gathered.dtype),
        compiler_params=params(8),
        cost_estimate=cost(0, 4 * gathered.size * 2),
        name="assemble",
    )(gathered)


def by_channel_kernel(in_ref, out_ref):
    peers, taps, rows, width = in_ref.shape
    depth, _, c_part, _ = out_ref.shape
    total = [sum(in_ref[p, tap].astype(jnp.float32) for p in range(peers)) for tap in range(taps)]
    turned = jnp.concatenate(total, axis=0).T.reshape(depth, Y_PARTS, c_part, taps * rows)
    blank = jnp.zeros((depth, c_part, LANES - Y_PARTS * rows), jnp.float32)
    for tap in range(taps):
        lanes = slice(tap * rows, (tap + 1) * rows)
        parts = [turned[:, low, :, lanes] for low in range(Y_PARTS)] + [blank]
        out_ref[:, tap] = jnp.concatenate(parts, axis=2).astype(out_ref.dtype)


def by_channel(parts, depth):
    taps, c_part = parts.shape[1], parts.shape[3] // (depth * Y_PARTS)
    return pl.pallas_call(
        by_channel_kernel,
        out_shape=struct((depth, taps, c_part, LANES), parts.dtype),
        compiler_params=params(16),
        cost_estimate=cost(0, 4 * parts.size),
        name="by_channel",
    )(parts)


def add_kernel(f_part, in_ref, out_ref):
    peers, taps, c_part, _ = in_ref.shape
    total = [sum(in_ref[p, tap].astype(jnp.float32) for p in range(peers)) for tap in range(taps)]
    blank = jnp.zeros((c_part, LANES - taps * f_part), jnp.float32)
    for low in range(Y_PARTS):
        for high in range(Y_PARTS):
            first = (low * Y_PARTS + high) * f_part
            parts = [t[:, first : first + f_part] for t in total] + [blank]
            out_ref[high * Y_PARTS + low] = jnp.concatenate(parts, axis=1).astype(out_ref.dtype)


def add_parts(parts, f_part):
    return pl.pallas_call(
        functools.partial(add_kernel, f_part),
        out_shape=struct((Y_PARTS * Y_PARTS,) + parts.shape[2:], parts.dtype),
        compiler_params=params(8),
        cost_estimate=cost(0, 4 * parts.size),
        name="add_parts",
    )(parts)


def finish_kernel(in_ref, _, out_ref):
    taps, _, f_part = out_ref.shape
    total = sum(in_ref[p].astype(jnp.float32) for p in range(in_ref.shape[0]))
    for tap in range(taps):
        out_ref[tap] = total[:, tap * f_part : (tap + 1) * f_part]


def finish(pieces, taps, f_part, after):
    return pl.pallas_call(
        finish_kernel,
        in_specs=[IN_VMEM, ANYWHERE],
        out_shape=struct((taps, pieces.shape[1], f_part), jnp.float32),
        compiler_params=params(8),
        cost_estimate=cost(0, 4 * pieces.size),
        name="finish",
    )(pieces, after)


def act_kernel(in_ref, _, *out_refs):
    for sample, out_ref in enumerate(out_refs):
        normed, _ = normalize(in_ref[sample])
        out_ref[...] = gelu_tanh(normed).astype(out_ref.dtype)


def activate(inputs, block, after):
    samples, bins, width = inputs.shape
    return pl.pallas_call(
        act_kernel,
        grid=(bins // block,),
        in_specs=[pl.BlockSpec((samples, block, width), lambda i: (0, i, 0)), ANYWHERE],
        out_specs=[pl.BlockSpec((block, width), lambda i: (i, 0))] * samples,
        out_shape=[struct((bins, width), inputs.dtype)] * samples,
        compiler_params=params(8),
        cost_estimate=cost(20 * inputs.size, 4 * inputs.size),
        name="activate",
    )(inputs, after)


def roles(yh):
    return (2 * yh, 1, 2 - 2 * yh)


def join_weights(sides, joined, point, yh, zl):
    for side, refs in enumerate(sides):
        for low, ref in enumerate(refs):
            pairs, far, span, lanes = ref.shape
            near, half = 2 * pairs, lanes // 4
            columns = slice(side * half, (side + 1) * half)
            for high in range(pairs):
                for zh in range(far):
                    first = (zh * near + (zl ^ (2 * high + low))) * span
                    rows = pl.ds(pl.multiple_of(first, span), span)
                    block = ref[high, zh]
                    for tap, role in enumerate(roles(yh)):
                        joined[role, rows, columns] = block[:, tap * half : (tap + 1) * half]
                    point[rows, columns] = block[:, 3 * half :]


def forward_kernel(scale, samples, at_ref, *refs):
    count = 3 * samples + 1
    far_refs, packed, refs = refs[:count], refs[count : count + 4], refs[count + 4 :]
    pre_ref, own_out, other_out, weights_out, refs = *refs[:4], refs[4:]
    acts, cot, weights, point, turned, own, other, sems = refs
    _, bins, width = cot.shape
    half = weights.shape[2] // CORES
    near_refs = [acts.at[i] for i in range(3 * samples)] + [cot]
    copies = [
        pltpu.make_async_copy(far_ref, near_ref, sems.at[i])
        for i, (far_ref, near_ref) in enumerate(zip(far_refs, near_refs))
    ]
    for sample in range(samples):
        for role in range(3):
            copies[role * samples + sample].start()
        if sample == 0:
            copies[count - 1].start()
    join_weights((packed[:2], packed[2:]), weights, point, at_ref[0], at_ref[1])
    keep = pltpu.make_async_copy(weights, weights_out, sems.at[count])
    keep.start()
    for sample in range(samples):
        handed, mid, partner = [acts.at[role * samples + sample] for role in range(3)]
        copies[sample].wait()
        shifted = dot(handed[...], weights[0], 1, 0).astype(jnp.bfloat16).astype(jnp.float32)
        copies[2 * samples + sample].wait()
        shifted += dot(partner[...], weights[2], 1, 0).astype(jnp.bfloat16).astype(jnp.float32)
        copies[samples + sample].wait()
        preact = shifted + dot(mid[...], weights[1], 1, 0)
        if sample == 0:
            copies[count - 1].wait()
        grad_inner = dot(cot[sample], point[...], 1, 0)
        grad_pre = grad_inner * gelu_slope(preact)
        pre_ref[sample] = grad_pre.astype(jnp.bfloat16)
        turned[:, pl.ds(sample * bins, bins)] = grad_pre.T.astype(jnp.bfloat16)
    sends = []
    for role, tap in enumerate(roles(at_ref[0])):
        block = acts[pl.ds(role * samples, samples)].reshape(samples * bins, width)
        term = dot(turned[...], block, 1, 0) * scale
        own[role] = term[:half].reshape(own.shape[1:])
        other[role] = term[half:].astype(jnp.bfloat16).reshape(other.shape[1:])
        for near_ref, far_ref in ((own, own_out), (other, other_out)):
            sem = sems.at[count + 1 + len(sends)]
            sends.append(pltpu.make_async_copy(near_ref.at[role], far_ref.at[:, tap], sem))
            sends[-1].start()
    for send in sends:
        send.wait()
    keep.wait()


def forward(at, acts, cotangent, own_w, other_w, scale):
    samples, bins, width = cotangent.shape
    hidden = CORES * own_w[0].shape[3] // 4
    half = (X_PARTS, 3, hidden // CORES // X_PARTS, width)
    count = 3 * samples
    return pl.pallas_call(
        functools.partial(forward_kernel, scale, samples),
        in_specs=[IN_SMEM] + [IN_HBM] * (count + 1) + [IN_VMEM] * 4,
        out_specs=[IN_VMEM] + [ANYWHERE] * 3,
        out_shape=[
            struct((samples, bins, hidden), jnp.bfloat16),
            struct(half, jnp.float32),
            struct(half, jnp.bfloat16),
            struct((3, width, hidden), jnp.bfloat16),
        ],
        scratch_shapes=[
            pltpu.VMEM((count, bins, width), jnp.bfloat16),
            pltpu.VMEM(cotangent.shape, jnp.bfloat16),
            pltpu.VMEM((3, width, hidden), jnp.bfloat16),
            pltpu.VMEM((width, hidden), jnp.bfloat16),
            pltpu.VMEM((hidden, samples * bins), jnp.bfloat16),
            pltpu.VMEM((3,) + half[:1] + half[2:], jnp.float32),
            pltpu.VMEM((3,) + half[:1] + half[2:], jnp.bfloat16),
            pltpu.SemaphoreType.DMA((count + 2 + 6,)),
        ],
        compiler_params=params(30),
        cost_estimate=cost(14 * samples * bins * width * hidden, 16 * samples * bins * width),
        name="forward",
    )(at, *[in_hbm(array) for array in (*acts, cotangent)], *own_w, *other_w)


def backward_kernel(in_ref, cot_ref, partner_ref, pre_ref, handed_ref, weights, out_ref, token_ref):
    token_ref[...] = jnp.zeros_like(token_ref)
    for sample in range(in_ref.shape[0]):
        grad_act = (
            dot(partner_ref[sample], weights[0], 1, 1)
            + dot(pre_ref[sample], weights[1], 1, 1)
            + dot(handed_ref[sample], weights[2], 1, 1)
        )
        normed, row_scale = normalize(in_ref[sample])
        grad_norm = grad_act * gelu_slope(normed)
        center = jnp.mean(grad_norm * normed, axis=-1, keepdims=True)
        grad = cot_ref[sample].astype(jnp.float32) + row_scale * (grad_norm - normed * center)
        out_ref[sample] = grad.astype(out_ref.dtype)


def backward(inputs, cotangent, partner, grad_pre, handed, weights, block):
    samples, bins, width = inputs.shape
    hidden = grad_pre.shape[2]
    wide = pl.BlockSpec((samples, block, width), lambda i: (0, i, 0))
    narrow = pl.BlockSpec((samples, block, hidden), lambda i: (0, i, 0))
    whole = pl.BlockSpec(weights.shape, lambda i: (0, 0, 0), pipeline_mode=pl.Buffered(1))
    return pl.pallas_call(
        backward_kernel,
        grid=(bins // block,),
        in_specs=[wide, wide, narrow, narrow, narrow, whole],
        out_specs=[wide, pl.BlockSpec((8, LANES), lambda i: (0, 0))],
        out_shape=[struct(inputs.shape, inputs.dtype), struct((8, LANES), jnp.float32)],
        compiler_params=params(24),
        cost_estimate=cost(6 * samples * bins * width * hidden, 16 * samples * bins * width),
        name="backward",
    )(in_hbm(inputs), in_hbm(cotangent), partner, grad_pre, handed, weights)


def exchanged(array):
    return lax.ppermute(array, "yh", [(0, 1), (1, 0)])


def handed_on(array):
    lower = [(Y_PARTS * i, Y_PARTS * (i + 1)) for i in range(X_PARTS - 1)]
    higher = [(Y_PARTS * (i + 1) + 1, Y_PARTS * i + 1) for i in range(X_PARTS - 1)]
    return lax.ppermute(array, ("x", "yh"), lower + higher)


def z_pair(array, bit):
    near = lax.axis_size("zl")
    return lax.ppermute(array, "zl", [(i, i ^ bit) for i in range(near)])


def other_core(array):
    return lax.ppermute(array, "core", [(0, 1), (1, 0)])


def body(inputs, conv_weight, point_weight, cotangent):
    samples, bins, width = inputs.shape
    taps, c_part, f_part = conv_weight.shape
    near, far = lax.axis_size("zl"), lax.axis_size("zh")
    depth = near * far
    blocks = X_PARTS * Y_PARTS
    devices = depth * Y_PARTS * blocks * CORES
    grad_scale = float(samples * bins * devices) ** (-0.5)
    at = jnp.stack([lax.axis_index("yh"), lax.axis_index("zl")]).astype(jnp.int32)

    packed = pack(in_hbm(conv_weight), in_hbm(point_weight), blocks * Y_PARTS)
    pieces = lax.all_to_all(packed, ("x", "yh", "yl"), 0, 0)

    mids = list(activate(in_hbm(inputs), 256, pieces))
    partners = [exchanged(mid) for mid in mids]

    part = lax.all_to_all(assemble(pieces, f_part, taps + 1)[:far], "zh", 0, 0)
    part = once(part, partners[0])
    handed = [handed_on(partners[0])]
    two = once(jnp.stack([part, z_pair(part, 2)]), corner(handed[0]), partners[1])
    handed.append(handed_on(partners[1]))
    other_two = other_core(two)
    last = once(z_pair(two, 1), corner(handed[1]))

    packed = (two, last, other_two, in_hbm(other_core(last)))

    grad_pre, own, other, weights = forward(
        at, handed + mids + partners, cotangent, packed[:2], packed[2:], grad_scale
    )

    def first_sums(own, other):
        pair = own + other.astype(jnp.float32)
        return lax.all_to_all(pair.astype(jnp.bfloat16), "x", 0, 0)

    other = other_core(other)
    grad_partner = exchanged(grad_pre)
    parts = held(first_sums, own, other)
    grad_handed = handed_on(once(grad_partner, corner(parts[0, 0])))

    parts = lax.all_to_all(by_channel(parts, depth), ("zh", "zl"), 0, 0)
    input_grad, token = backward(
        inputs, cotangent, grad_partner, grad_pre, grad_handed, weights, 256
    )
    sums = add_parts(parts, f_part)
    conv_grad = finish(lax.all_to_all(sums, ("yh", "yl"), 0, 0), taps, f_part, token)
    return (input_grad, conv_grad)


def solution(mesh):
    depth = mesh.shape["dp"] // Y_PARTS
    fine = Mesh(
        mesh.devices.reshape(depth // Z_PARTS, Z_PARTS, Y_PARTS, X_PARTS, Y_PARTS, CORES),
        ("zh", "zl", "yl", "x", "yh", "core"),
    )
    dp, seq = ("zh", "zl", "yl"), ("x", "yh", "core")
    return jax.shard_map(
        body,
        mesh=fine,
        in_specs=(P(dp, seq, None), P(None, dp, seq), P(seq, dp), P(dp, seq, None)),
        out_specs=(P(dp, seq, None), P(None, dp, seq)),
        check_vma=False,
    )
```

```python
import functools

import jax
import jax.numpy as jnp
from jax import lax
from jax.experimental import pallas as pl
from jax.experimental.pallas import tpu as pltpu
from jax.sharding import Mesh
from jax.sharding import PartitionSpec as P

LANES = 128
SUBLANES = 8
X_PARTS, Y_PARTS, Z_PARTS, CORES = 4, 2, 4, 2
MIB = 1024 * 1024

EPSILON = 1e-06
GELU_SCALE = 0.7978845608028654
GELU_CUBIC = 0.044715


def gelu_tanh(values):
    return (
        0.5
        * values
        * (1.0 + jnp.tanh(GELU_SCALE * (values + GELU_CUBIC * values * values * values)))
    )


def gelu_slope(values):
    tangent = jnp.tanh(GELU_SCALE * (values + GELU_CUBIC * values * values * values))
    return 0.5 * (1.0 + tangent) + 0.5 * values * (1.0 - tangent * tangent) * GELU_SCALE * (
        1.0 + 3.0 * GELU_CUBIC * values * values
    )


def dot(left, right, left_dim, right_dim):
    return lax.dot_general(
        left, right, (((left_dim,), (right_dim,)), ((), ())), preferred_element_type=jnp.float32
    )


def normalize(values):
    floats = values.astype(jnp.float32)
    row_scale = lax.rsqrt(jnp.mean(floats * floats, axis=-1, keepdims=True) + EPSILON)
    return floats * row_scale, row_scale


def params(mib):
    return pltpu.CompilerParams(vmem_limit_bytes=mib * MIB)


def struct(shape, dtype):
    return jax.ShapeDtypeStruct(shape, dtype)


def cost(flops, nbytes):
    return pl.CostEstimate(flops=flops, bytes_accessed=nbytes, transcendentals=0)


ANYWHERE = pl.BlockSpec(memory_space=pl.ANY)
IN_VMEM = pl.BlockSpec(memory_space=pltpu.VMEM)
IN_HBM = pl.BlockSpec(memory_space=pltpu.HBM)
IN_SMEM = pl.BlockSpec(memory_space=pltpu.SMEM)


def in_hbm(array):
    return pltpu.with_memory_space_constraint(array, pltpu.HBM)


def once_kernel(in_ref, *refs):
    refs[-1][...] = in_ref[...]


def once(array, *after):
    return pl.pallas_call(
        once_kernel,
        in_specs=[IN_VMEM] + [ANYWHERE] * len(after),
        out_shape=struct(array.shape, array.dtype),
        compiler_params=params(8),
        cost_estimate=cost(0, 4 * array.size),
        name="once",
    )(array, *after)


def corner(array):
    return array[: 2 * SUBLANES, :LANES]


def held(stage, *args):
    def blank(*args):
        return jnp.zeros(out.shape, out.dtype)

    out = jax.eval_shape(stage, *args)
    return lax.cond(lax.axis_index("x") < X_PARTS, stage, blank, *args)


def pack_kernel(conv_ref, point_ref, out_ref):
    taps, c_part, f_part = conv_ref.shape
    pieces = [conv_ref[tap].astype(jnp.float32) for tap in range(taps)]
    pieces.append(point_ref[...].astype(jnp.float32).T)
    pieces.append(jnp.zeros((c_part, LANES - (taps + 1) * f_part), jnp.float32))
    packed = jnp.concatenate(pieces, axis=1).astype(out_ref.dtype)
    out_ref[...] = jnp.broadcast_to(packed[None], out_ref.shape)


def pack(conv_weight, point_weight, peers):
    c_part = conv_weight.shape[1]
    return pl.pallas_call(
        pack_kernel,
        out_shape=struct((peers, c_part, LANES), conv_weight.dtype),
        compiler_params=params(8),
        cost_estimate=cost(0, 2 * peers * c_part * LANES),
        name="pack",
    )(conv_weight, point_weight)


def assemble_kernel(f_part, taps, in_ref, out_ref):
    blocks = in_ref.shape[0] // Y_PARTS
    for low in range(Y_PARTS):
        pieces = [in_ref[Y_PARTS * block + low].astype(jnp.float32) for block in range(blocks)]
        rows = jnp.concatenate(
            [
                piece[:, tap * f_part : (tap + 1) * f_part]
                for tap in range(taps)
                for piece in pieces
            ],
            axis=1,
        )
        span = rows.shape[0]
        for copy in range(Z_PARTS):
            out_ref[copy, pl.ds(low * span, span), :] = rows.astype(out_ref.dtype)


def assemble(gathered, f_part, taps):
    peers, c_part, _ = gathered.shape
    lanes = peers // Y_PARTS * taps * f_part
    return pl.pallas_call(
        functools.partial(assemble_kernel, f_part, taps),
        out_shape=struct((Z_PARTS, Y_PARTS * c_part, lanes), gathered.dtype),
        compiler_params=params(8),
        cost_estimate=cost(0, 4 * gathered.size * 2),
        name="assemble",
    )(gathered)


def by_channel_kernel(in_ref, out_ref):
    peers, taps, rows, width = in_ref.shape
    depth, _, c_part, _ = out_ref.shape
    total = [sum(in_ref[p, tap].astype(jnp.float32) for p in range(peers)) for tap in range(taps)]
    turned = jnp.concatenate(total, axis=0).T.reshape(depth, Y_PARTS, c_part, taps * rows)
    blank = jnp.zeros((depth, c_part, LANES - Y_PARTS * rows), jnp.float32)
    for tap in range(taps):
        lanes = slice(tap * rows, (tap + 1) * rows)
        parts = [turned[:, low, :, lanes] for low in range(Y_PARTS)] + [blank]
        out_ref[:, tap] = jnp.concatenate(parts, axis=2).astype(out_ref.dtype)


def by_channel(parts, depth):
    taps, c_part = parts.shape[1], parts.shape[3] // (depth * Y_PARTS)
    return pl.pallas_call(
        by_channel_kernel,
        out_shape=struct((depth, taps, c_part, LANES), parts.dtype),
        compiler_params=params(16),
        cost_estimate=cost(0, 4 * parts.size),
        name="by_channel",
    )(parts)


def add_kernel(f_part, in_ref, out_ref):
    peers, taps, c_part, _ = in_ref.shape
    total = [sum(in_ref[p, tap].astype(jnp.float32) for p in range(peers)) for tap in range(taps)]
    blank = jnp.zeros((c_part, LANES - taps * f_part), jnp.float32)
    for low in range(Y_PARTS):
        for high in range(Y_PARTS):
            first = (low * Y_PARTS + high) * f_part
            parts = [t[:, first : first + f_part] for t in total] + [blank]
            out_ref[high * Y_PARTS + low] = jnp.concatenate(parts, axis=1).astype(out_ref.dtype)


def add_parts(parts, f_part):
    return pl.pallas_call(
        functools.partial(add_kernel, f_part),
        out_shape=struct((Y_PARTS * Y_PARTS,) + parts.shape[2:], parts.dtype),
        compiler_params=params(8),
        cost_estimate=cost(0, 4 * parts.size),
        name="add_parts",
    )(parts)


def finish_kernel(in_ref, _, out_ref):
    taps, _, f_part = out_ref.shape
    total = sum(in_ref[p].astype(jnp.float32) for p in range(in_ref.shape[0]))
    for tap in range(taps):
        out_ref[tap] = total[:, tap * f_part : (tap + 1) * f_part]


def finish(pieces, taps, f_part, after):
    return pl.pallas_call(
        finish_kernel,
        in_specs=[IN_VMEM, ANYWHERE],
        out_shape=struct((taps, pieces.shape[1], f_part), jnp.float32),
        compiler_params=params(8),
        cost_estimate=cost(0, 4 * pieces.size),
        name="finish",
    )(pieces, after)


def act_kernel(in_ref, _, *out_refs):
    for sample, out_ref in enumerate(out_refs):
        normed, _ = normalize(in_ref[sample])
        out_ref[...] = gelu_tanh(normed).astype(out_ref.dtype)


def activate(inputs, block, after):
    samples, bins, width = inputs.shape
    return pl.pallas_call(
        act_kernel,
        grid=(bins // block,),
        in_specs=[pl.BlockSpec((samples, block, width), lambda i: (0, i, 0)), ANYWHERE],
        out_specs=[pl.BlockSpec((block, width), lambda i: (i, 0))] * samples,
        out_shape=[struct((bins, width), inputs.dtype)] * samples,
        compiler_params=params(8),
        cost_estimate=cost(20 * inputs.size, 4 * inputs.size),
        name="activate",
    )(inputs, after)


def roles(yh):
    return (2 * yh, 1, 2 - 2 * yh)


def join_weights(sides, joined, point, yh, zl):
    for side, refs in enumerate(sides):
        for low, ref in enumerate(refs):
            pairs, far, span, lanes = ref.shape
            near, half = 2 * pairs, lanes // 4
            columns = slice(side * half, (side + 1) * half)
            for high in range(pairs):
                for zh in range(far):
                    first = (zh * near + (zl ^ (2 * high + low))) * span
                    rows = pl.ds(pl.multiple_of(first, span), span)
                    block = ref[high, zh]
                    for tap, role in enumerate(roles(yh)):
                        joined[role, rows, columns] = block[:, tap * half : (tap + 1) * half]
                    point[rows, columns] = block[:, 3 * half :]


def forward_kernel(scale, samples, at_ref, *refs):
    count = 3 * samples + 1
    far_refs, packed, refs = refs[:count], refs[count : count + 4], refs[count + 4 :]
    pre_ref, own_out, other_out, weights_out, acts, cot, weights, point, turned, sems = refs
    _, bins, width = cot.shape
    half = weights.shape[2] // CORES
    near_refs = [acts.at[i] for i in range(3 * samples)] + [cot]
    copies = [
        pltpu.make_async_copy(far_ref, near_ref, sems.at[i])
        for i, (far_ref, near_ref) in enumerate(zip(far_refs, near_refs))
    ]
    for sample in range(samples):
        for role in range(3):
            copies[role * samples + sample].start()
        if sample == 0:
            copies[count - 1].start()
    join_weights((packed[:2], packed[2:]), weights, point, at_ref[0], at_ref[1])
    keep = pltpu.make_async_copy(weights, weights_out, sems.at[count])
    keep.start()
    for sample in range(samples):
        for role in range(3):
            copies[role * samples + sample].wait()
        if sample == 0:
            copies[count - 1].wait()
        handed, mid, partner = [acts[role * samples + sample] for role in range(3)]
        shifted = dot(handed, weights[0], 1, 0).astype(jnp.bfloat16).astype(jnp.float32)
        shifted += dot(partner, weights[2], 1, 0).astype(jnp.bfloat16).astype(jnp.float32)
        preact = shifted + dot(mid, weights[1], 1, 0)
        grad_inner = dot(cot[sample], point[...], 1, 0)
        grad_pre = grad_inner * gelu_slope(preact)
        pre_ref[sample] = grad_pre.astype(jnp.bfloat16)
        turned[:, pl.ds(sample * bins, bins)] = grad_pre.T.astype(jnp.bfloat16)
    for role, tap in enumerate(roles(at_ref[0])):
        block = acts[pl.ds(role * samples, samples)].reshape(samples * bins, width)
        term = dot(turned[...], block, 1, 0) * scale
        own_out[:, tap] = term[:half].reshape(own_out.shape[0], -1, width)
        other = term[half:].astype(jnp.bfloat16)
        other_out[:, tap] = other.reshape(other_out.shape[0], -1, width)
    keep.wait()


def forward(at, acts, cotangent, own_w, other_w, scale):
    samples, bins, width = cotangent.shape
    hidden = CORES * own_w[0].shape[3] // 4
    half = (X_PARTS, 3, hidden // CORES // X_PARTS, width)
    count = 3 * samples
    return pl.pallas_call(
        functools.partial(forward_kernel, scale, samples),
        in_specs=[IN_SMEM] + [IN_HBM] * (count + 1) + [IN_VMEM] * 4,
        out_specs=[IN_VMEM] * 3 + [IN_HBM],
        out_shape=[
            struct((samples, bins, hidden), jnp.bfloat16),
            struct(half, jnp.float32),
            struct(half, jnp.bfloat16),
            struct((3, width, hidden), jnp.bfloat16),
        ],
        scratch_shapes=[
            pltpu.VMEM((count, bins, width), jnp.bfloat16),
            pltpu.VMEM(cotangent.shape, jnp.bfloat16),
            pltpu.VMEM((3, width, hidden), jnp.bfloat16),
            pltpu.VMEM((width, hidden), jnp.bfloat16),
            pltpu.VMEM((hidden, samples * bins), jnp.bfloat16),
            pltpu.SemaphoreType.DMA((count + 2,)),
        ],
        compiler_params=params(30),
        cost_estimate=cost(14 * samples * bins * width * hidden, 16 * samples * bins * width),
        name="forward",
    )(at, *[in_hbm(array) for array in (*acts, cotangent)], *own_w, *other_w)


def backward_kernel(in_ref, cot_ref, partner_ref, pre_ref, handed_ref, weights, out_ref, token_ref):
    token_ref[...] = jnp.zeros_like(token_ref)
    for sample in range(in_ref.shape[0]):
        grad_act = (
            dot(partner_ref[sample], weights[0], 1, 1)
            + dot(pre_ref[sample], weights[1], 1, 1)
            + dot(handed_ref[sample], weights[2], 1, 1)
        )
        normed, row_scale = normalize(in_ref[sample])
        grad_norm = grad_act * gelu_slope(normed)
        center = jnp.mean(grad_norm * normed, axis=-1, keepdims=True)
        grad = cot_ref[sample].astype(jnp.float32) + row_scale * (grad_norm - normed * center)
        out_ref[sample] = grad.astype(out_ref.dtype)


def backward(inputs, cotangent, partner, grad_pre, handed, weights, block):
    samples, bins, width = inputs.shape
    hidden = grad_pre.shape[2]
    wide = pl.BlockSpec((samples, block, width), lambda i: (0, i, 0))
    narrow = pl.BlockSpec((samples, block, hidden), lambda i: (0, i, 0))
    whole = pl.BlockSpec(weights.shape, lambda i: (0, 0, 0), pipeline_mode=pl.Buffered(1))
    return pl.pallas_call(
        backward_kernel,
        grid=(bins // block,),
        in_specs=[wide, wide, narrow, narrow, narrow, whole],
        out_specs=[wide, pl.BlockSpec((8, LANES), lambda i: (0, 0))],
        out_shape=[struct(inputs.shape, inputs.dtype), struct((8, LANES), jnp.float32)],
        compiler_params=params(24),
        cost_estimate=cost(6 * samples * bins * width * hidden, 16 * samples * bins * width),
        name="backward",
    )(in_hbm(inputs), in_hbm(cotangent), partner, grad_pre, handed, weights)


def exchanged(array):
    return lax.ppermute(array, "yh", [(0, 1), (1, 0)])


def handed_on(array):
    lower = [(Y_PARTS * i, Y_PARTS * (i + 1)) for i in range(X_PARTS - 1)]
    higher = [(Y_PARTS * (i + 1) + 1, Y_PARTS * i + 1) for i in range(X_PARTS - 1)]
    return lax.ppermute(array, ("x", "yh"), lower + higher)


def z_pair(array, bit):
    near = lax.axis_size("zl")
    return lax.ppermute(array, "zl", [(i, i ^ bit) for i in range(near)])


def other_core(array):
    return lax.ppermute(array, "core", [(0, 1), (1, 0)])


def body(inputs, conv_weight, point_weight, cotangent):
    samples, bins, width = inputs.shape
    taps, c_part, f_part = conv_weight.shape
    near, far = lax.axis_size("zl"), lax.axis_size("zh")
    depth = near * far
    blocks = X_PARTS * Y_PARTS
    devices = depth * Y_PARTS * blocks * CORES
    grad_scale = float(samples * bins * devices) ** (-0.5)
    at = jnp.stack([lax.axis_index("yh"), lax.axis_index("zl")]).astype(jnp.int32)

    packed = pack(in_hbm(conv_weight), in_hbm(point_weight), blocks * Y_PARTS)
    pieces = lax.all_to_all(packed, ("x", "yh", "yl"), 0, 0)

    mids = list(activate(in_hbm(inputs), 256, pieces))
    partners = [exchanged(mid) for mid in mids]

    part = lax.all_to_all(assemble(pieces, f_part, taps + 1)[:far], "zh", 0, 0)
    part = once(part, partners[0])
    handed = [handed_on(partners[0])]
    two = once(jnp.stack([part, z_pair(part, 2)]), corner(handed[0]), partners[1])
    handed.append(handed_on(partners[1]))
    other_two = other_core(two)
    last = once(z_pair(two, 1), corner(handed[1]))

    packed = (two, last, in_hbm(other_two), in_hbm(other_core(last)))

    grad_pre, own, other, weights = forward(
        at, handed + mids + partners, cotangent, packed[:2], packed[2:], grad_scale
    )

    def first_sums(own, other):
        return (own + other.astype(jnp.float32)).astype(jnp.bfloat16)

    other = other_core(other)
    grad_partner = exchanged(grad_pre)
    parts = lax.all_to_all(held(first_sums, own, other), "x", 0, 0)
    grad_handed = handed_on(once(grad_partner, parts))

    parts = lax.all_to_all(by_channel(parts, depth), ("zh", "zl"), 0, 0)
    input_grad, token = backward(
        inputs, cotangent, grad_partner, grad_pre, grad_handed, weights, 256
    )
    sums = add_parts(parts, f_part)
    conv_grad = finish(lax.all_to_all(sums, ("yh", "yl"), 0, 0), taps, f_part, token)
    return (input_grad, conv_grad)


def solution(mesh):
    depth = mesh.shape["dp"] // Y_PARTS
    fine = Mesh(
        mesh.devices.reshape(depth // Z_PARTS, Z_PARTS, Y_PARTS, X_PARTS, Y_PARTS, CORES),
        ("zh", "zl", "yl", "x", "yh", "core"),
    )
    dp, seq = ("zh", "zl", "yl"), ("x", "yh", "core")
    return jax.shard_map(
        body,
        mesh=fine,
        in_specs=(P(dp, seq, None), P(None, dp, seq), P(seq, dp), P(dp, seq, None)),
        out_specs=(P(dp, seq, None), P(None, dp, seq)),
        check_vma=False,
    )
```

```python
import functools

import jax
import jax.numpy as jnp
from jax import lax
from jax.experimental import pallas as pl
from jax.experimental.pallas import tpu as pltpu
from jax.sharding import Mesh
from jax.sharding import PartitionSpec as P

LANES = 128
SUBLANES = 8
X_PARTS, Y_PARTS, Z_PARTS, CORES = 4, 2, 4, 2
MIB = 1024 * 1024

EPSILON = 1e-06
GELU_SCALE = 0.7978845608028654
GELU_CUBIC = 0.044715


def gelu_tanh(values):
    return (
        0.5
        * values
        * (1.0 + jnp.tanh(GELU_SCALE * (values + GELU_CUBIC * values * values * values)))
    )


def gelu_slope(values):
    tangent = jnp.tanh(GELU_SCALE * (values + GELU_CUBIC * values * values * values))
    return 0.5 * (1.0 + tangent) + 0.5 * values * (1.0 - tangent * tangent) * GELU_SCALE * (
        1.0 + 3.0 * GELU_CUBIC * values * values
    )


def dot(left, right, left_dim, right_dim):
    return lax.dot_general(
        left, right, (((left_dim,), (right_dim,)), ((), ())), preferred_element_type=jnp.float32
    )


def normalize(values):
    floats = values.astype(jnp.float32)
    row_scale = lax.rsqrt(jnp.mean(floats * floats, axis=-1, keepdims=True) + EPSILON)
    return floats * row_scale, row_scale


def params(mib):
    return pltpu.CompilerParams(vmem_limit_bytes=mib * MIB)


def struct(shape, dtype):
    return jax.ShapeDtypeStruct(shape, dtype)


def cost(flops, nbytes):
    return pl.CostEstimate(flops=flops, bytes_accessed=nbytes, transcendentals=0)


ANYWHERE = pl.BlockSpec(memory_space=pl.ANY)
IN_VMEM = pl.BlockSpec(memory_space=pltpu.VMEM)
IN_HBM = pl.BlockSpec(memory_space=pltpu.HBM)
IN_SMEM = pl.BlockSpec(memory_space=pltpu.SMEM)


def in_hbm(array):
    return pltpu.with_memory_space_constraint(array, pltpu.HBM)


def once_kernel(in_ref, *refs):
    refs[-1][...] = in_ref[...]


def once(array, *after):
    return pl.pallas_call(
        once_kernel,
        in_specs=[IN_VMEM] + [ANYWHERE] * len(after),
        out_shape=struct(array.shape, array.dtype),
        compiler_params=params(8),
        cost_estimate=cost(0, 4 * array.size),
        name="once",
    )(array, *after)


def corner(array):
    return array[: 2 * SUBLANES, :LANES]


def held(stage, *args):
    def blank(*args):
        return jnp.zeros(out.shape, out.dtype)

    out = jax.eval_shape(stage, *args)
    return lax.cond(lax.axis_index("x") < X_PARTS, stage, blank, *args)


def pack_kernel(conv_ref, point_ref, out_ref):
    taps, c_part, f_part = conv_ref.shape
    pieces = [conv_ref[tap].astype(jnp.float32) for tap in range(taps)]
    pieces.append(point_ref[...].astype(jnp.float32).T)
    pieces.append(jnp.zeros((c_part, LANES - (taps + 1) * f_part), jnp.float32))
    packed = jnp.concatenate(pieces, axis=1).astype(out_ref.dtype)
    out_ref[...] = jnp.broadcast_to(packed[None], out_ref.shape)


def pack(conv_weight, point_weight, peers):
    c_part = conv_weight.shape[1]
    return pl.pallas_call(
        pack_kernel,
        out_shape=struct((peers, c_part, LANES), conv_weight.dtype),
        compiler_params=params(8),
        cost_estimate=cost(0, 2 * peers * c_part * LANES),
        name="pack",
    )(conv_weight, point_weight)


def assemble_kernel(f_part, taps, in_ref, out_ref):
    blocks = in_ref.shape[0] // Y_PARTS
    for low in range(Y_PARTS):
        pieces = [in_ref[Y_PARTS * block + low].astype(jnp.float32) for block in range(blocks)]
        rows = jnp.concatenate(
            [
                piece[:, tap * f_part : (tap + 1) * f_part]
                for tap in range(taps)
                for piece in pieces
            ],
            axis=1,
        )
        span = rows.shape[0]
        for copy in range(Z_PARTS):
            out_ref[copy, pl.ds(low * span, span), :] = rows.astype(out_ref.dtype)


def assemble(gathered, f_part, taps):
    peers, c_part, _ = gathered.shape
    lanes = peers // Y_PARTS * taps * f_part
    return pl.pallas_call(
        functools.partial(assemble_kernel, f_part, taps),
        out_shape=struct((Z_PARTS, Y_PARTS * c_part, lanes), gathered.dtype),
        compiler_params=params(8),
        cost_estimate=cost(0, 4 * gathered.size * 2),
        name="assemble",
    )(gathered)


def by_channel_kernel(in_ref, out_ref):
    peers, taps, rows, width = in_ref.shape
    depth, _, c_part, _ = out_ref.shape
    total = [sum(in_ref[p, tap].astype(jnp.float32) for p in range(peers)) for tap in range(taps)]
    turned = jnp.concatenate(total, axis=0).T.reshape(depth, Y_PARTS, c_part, taps * rows)
    blank = jnp.zeros((depth, c_part, LANES - Y_PARTS * rows), jnp.float32)
    for tap in range(taps):
        lanes = slice(tap * rows, (tap + 1) * rows)
        parts = [turned[:, low, :, lanes] for low in range(Y_PARTS)] + [blank]
        out_ref[:, tap] = jnp.concatenate(parts, axis=2).astype(out_ref.dtype)


def by_channel(parts, depth):
    taps, c_part = parts.shape[1], parts.shape[3] // (depth * Y_PARTS)
    return pl.pallas_call(
        by_channel_kernel,
        out_shape=struct((depth, taps, c_part, LANES), parts.dtype),
        compiler_params=params(16),
        cost_estimate=cost(0, 4 * parts.size),
        name="by_channel",
    )(parts)


def add_kernel(f_part, in_ref, out_ref):
    peers, taps, c_part, _ = in_ref.shape
    total = [sum(in_ref[p, tap].astype(jnp.float32) for p in range(peers)) for tap in range(taps)]
    blank = jnp.zeros((c_part, LANES - taps * f_part), jnp.float32)
    for low in range(Y_PARTS):
        for high in range(Y_PARTS):
            first = (low * Y_PARTS + high) * f_part
            parts = [t[:, first : first + f_part] for t in total] + [blank]
            out_ref[high * Y_PARTS + low] = jnp.concatenate(parts, axis=1).astype(out_ref.dtype)


def add_parts(parts, f_part):
    return pl.pallas_call(
        functools.partial(add_kernel, f_part),
        out_shape=struct((Y_PARTS * Y_PARTS,) + parts.shape[2:], parts.dtype),
        compiler_params=params(8),
        cost_estimate=cost(0, 4 * parts.size),
        name="add_parts",
    )(parts)


def finish_kernel(in_ref, _, out_ref):
    taps, _, f_part = out_ref.shape
    total = sum(in_ref[p].astype(jnp.float32) for p in range(in_ref.shape[0]))
    for tap in range(taps):
        out_ref[tap] = total[:, tap * f_part : (tap + 1) * f_part]


def finish(pieces, taps, f_part, after):
    return pl.pallas_call(
        finish_kernel,
        in_specs=[IN_VMEM, ANYWHERE],
        out_shape=struct((taps, pieces.shape[1], f_part), jnp.float32),
        compiler_params=params(8),
        cost_estimate=cost(0, 4 * pieces.size),
        name="finish",
    )(pieces, after)


def act_kernel(in_ref, _, *out_refs):
    for sample, out_ref in enumerate(out_refs):
        normed, _ = normalize(in_ref[sample])
        out_ref[...] = gelu_tanh(normed).astype(out_ref.dtype)


def activate(inputs, block, after):
    samples, bins, width = inputs.shape
    return pl.pallas_call(
        act_kernel,
        grid=(bins // block,),
        in_specs=[pl.BlockSpec((samples, block, width), lambda i: (0, i, 0)), ANYWHERE],
        out_specs=[pl.BlockSpec((block, width), lambda i: (i, 0))] * samples,
        out_shape=[struct((bins, width), inputs.dtype)] * samples,
        compiler_params=params(8),
        cost_estimate=cost(20 * inputs.size, 4 * inputs.size),
        name="activate",
    )(inputs, after)


def roles(yh):
    return (2 * yh, 1, 2 - 2 * yh)


def join_weights(sides, joined, point, yh, zl):
    for side, refs in enumerate(sides):
        for low, ref in enumerate(refs):
            pairs, far, span, lanes = ref.shape
            near, half = 2 * pairs, lanes // 4
            columns = slice(side * half, (side + 1) * half)
            for high in range(pairs):
                for zh in range(far):
                    first = (zh * near + (zl ^ (2 * high + low))) * span
                    rows = pl.ds(pl.multiple_of(first, span), span)
                    block = ref[high, zh]
                    for tap, role in enumerate(roles(yh)):
                        joined[role, rows, columns] = block[:, tap * half : (tap + 1) * half]
                    point[rows, columns] = block[:, 3 * half :]


def forward_kernel(scale, samples, at_ref, *refs):
    count = 3 * samples + 1
    far_refs, packed, refs = refs[:count], refs[count : count + 4], refs[count + 4 :]
    pre_ref, own_out, other_out, weights_out, acts, cot, weights, point, turned, sems = refs
    _, bins, width = cot.shape
    half = weights.shape[2] // CORES
    near_refs = [acts.at[i] for i in range(3 * samples)] + [cot]
    copies = [
        pltpu.make_async_copy(far_ref, near_ref, sems.at[i])
        for i, (far_ref, near_ref) in enumerate(zip(far_refs, near_refs))
    ]
    for sample in range(samples):
        for role in range(3):
            copies[role * samples + sample].start()
        if sample == 0:
            copies[count - 1].start()
    join_weights((packed[:2], packed[2:]), weights, point, at_ref[0], at_ref[1])
    keep = pltpu.make_async_copy(weights, weights_out, sems.at[count])
    keep.start()
    for sample in range(samples):
        for role in range(3):
            copies[role * samples + sample].wait()
        if sample == 0:
            copies[count - 1].wait()
        handed, mid, partner = [acts[role * samples + sample] for role in range(3)]
        shifted = dot(handed, weights[0], 1, 0).astype(jnp.bfloat16).astype(jnp.float32)
        shifted += dot(partner, weights[2], 1, 0).astype(jnp.bfloat16).astype(jnp.float32)
        preact = shifted + dot(mid, weights[1], 1, 0)
        grad_inner = dot(cot[sample], point[...], 1, 0)
        grad_pre = grad_inner * gelu_slope(preact)
        pre_ref[sample] = grad_pre.astype(jnp.bfloat16)
        turned[:, pl.ds(sample * bins, bins)] = grad_pre.T.astype(jnp.bfloat16)
    for role, tap in enumerate(roles(at_ref[0])):
        block = acts[pl.ds(role * samples, samples)].reshape(samples * bins, width)
        term = dot(turned[...], block, 1, 0) * scale
        own_out[:, tap] = term[:half].reshape(own_out.shape[0], -1, width)
        other = term[half:].astype(jnp.bfloat16)
        other_out[:, tap] = other.reshape(other_out.shape[0], -1, width)
    keep.wait()


def forward(at, acts, cotangent, own_w, other_w, scale):
    samples, bins, width = cotangent.shape
    hidden = CORES * own_w[0].shape[3] // 4
    half = (X_PARTS, 3, hidden // CORES // X_PARTS, width)
    count = 3 * samples
    return pl.pallas_call(
        functools.partial(forward_kernel, scale, samples),
        in_specs=[IN_SMEM] + [IN_HBM] * (count + 1) + [IN_VMEM] * 4,
        out_specs=[IN_VMEM] * 3 + [IN_HBM],
        out_shape=[
            struct((samples, bins, hidden), jnp.bfloat16),
            struct(half, jnp.float32),
            struct(half, jnp.bfloat16),
            struct((3, width, hidden), jnp.bfloat16),
        ],
        scratch_shapes=[
            pltpu.VMEM((count, bins, width), jnp.bfloat16),
            pltpu.VMEM(cotangent.shape, jnp.bfloat16),
            pltpu.VMEM((3, width, hidden), jnp.bfloat16),
            pltpu.VMEM((width, hidden), jnp.bfloat16),
            pltpu.VMEM((hidden, samples * bins), jnp.bfloat16),
            pltpu.SemaphoreType.DMA((count + 2,)),
        ],
        compiler_params=params(30),
        cost_estimate=cost(14 * samples * bins * width * hidden, 16 * samples * bins * width),
        name="forward",
    )(at, *[in_hbm(array) for array in (*acts, cotangent)], *own_w, *other_w)


def backward_kernel(in_ref, cot_ref, partner_ref, pre_ref, handed_ref, weights, out_ref, token_ref):
    token_ref[...] = jnp.zeros_like(token_ref)
    for sample in range(in_ref.shape[0]):
        grad_act = (
            dot(partner_ref[sample], weights[0], 1, 1)
            + dot(pre_ref[sample], weights[1], 1, 1)
            + dot(handed_ref[sample], weights[2], 1, 1)
        )
        normed, row_scale = normalize(in_ref[sample])
        grad_norm = grad_act * gelu_slope(normed)
        center = jnp.mean(grad_norm * normed, axis=-1, keepdims=True)
        grad = cot_ref[sample].astype(jnp.float32) + row_scale * (grad_norm - normed * center)
        out_ref[sample] = grad.astype(out_ref.dtype)


def backward(inputs, cotangent, partner, grad_pre, handed, weights, block):
    samples, bins, width = inputs.shape
    hidden = grad_pre.shape[2]
    wide = pl.BlockSpec((samples, block, width), lambda i: (0, i, 0))
    narrow = pl.BlockSpec((samples, block, hidden), lambda i: (0, i, 0))
    whole = pl.BlockSpec(weights.shape, lambda i: (0, 0, 0), pipeline_mode=pl.Buffered(1))
    return pl.pallas_call(
        backward_kernel,
        grid=(bins // block,),
        in_specs=[wide, wide, narrow, narrow, narrow, whole],
        out_specs=[wide, pl.BlockSpec((8, LANES), lambda i: (0, 0))],
        out_shape=[struct(inputs.shape, inputs.dtype), struct((8, LANES), jnp.float32)],
        compiler_params=params(24),
        cost_estimate=cost(6 * samples * bins * width * hidden, 16 * samples * bins * width),
        name="backward",
    )(in_hbm(inputs), in_hbm(cotangent), partner, grad_pre, handed, weights)


def exchanged(array):
    return lax.ppermute(array, "yh", [(0, 1), (1, 0)])


def handed_on(array):
    lower = [(Y_PARTS * i, Y_PARTS * (i + 1)) for i in range(X_PARTS - 1)]
    higher = [(Y_PARTS * (i + 1) + 1, Y_PARTS * i + 1) for i in range(X_PARTS - 1)]
    return lax.ppermute(array, ("x", "yh"), lower + higher)


def z_pair(array, bit):
    near = lax.axis_size("zl")
    return lax.ppermute(array, "zl", [(i, i ^ bit) for i in range(near)])


def other_core(array):
    return lax.ppermute(array, "core", [(0, 1), (1, 0)])


def body(inputs, conv_weight, point_weight, cotangent):
    samples, bins, width = inputs.shape
    taps, c_part, f_part = conv_weight.shape
    near, far = lax.axis_size("zl"), lax.axis_size("zh")
    depth = near * far
    blocks = X_PARTS * Y_PARTS
    devices = depth * Y_PARTS * blocks * CORES
    grad_scale = float(samples * bins * devices) ** (-0.5)
    at = jnp.stack([lax.axis_index("yh"), lax.axis_index("zl")]).astype(jnp.int32)

    packed = pack(in_hbm(conv_weight), in_hbm(point_weight), blocks * Y_PARTS)
    pieces = lax.all_to_all(packed, ("x", "yh", "yl"), 0, 0)

    mids = list(activate(in_hbm(inputs), 256, pieces))
    partners = [exchanged(mid) for mid in mids]

    part = lax.all_to_all(assemble(pieces, f_part, taps + 1)[:far], "zh", 0, 0)
    part = once(part, partners[0])
    handed = [handed_on(partners[0])]
    two = once(jnp.stack([part, z_pair(part, 2)]), corner(handed[0]), partners[1])
    handed.append(handed_on(partners[1]))
    other_two = other_core(two)
    last = once(z_pair(two, 1), corner(handed[1]))

    packed = (two, last, other_two, in_hbm(other_core(last)))

    grad_pre, own, other, weights = forward(
        at, handed + mids + partners, cotangent, packed[:2], packed[2:], grad_scale
    )

    def first_sums(own, other):
        pair = own + other.astype(jnp.float32)
        return lax.all_to_all(pair.astype(jnp.bfloat16), "x", 0, 0)

    other = other_core(other)
    grad_partner = exchanged(grad_pre)
    parts = held(first_sums, own, other)
    grad_handed = handed_on(once(grad_partner, parts))

    parts = lax.all_to_all(by_channel(parts, depth), ("zh", "zl"), 0, 0)
    input_grad, token = backward(
        inputs, cotangent, grad_partner, grad_pre, grad_handed, weights, 256
    )
    sums = add_parts(parts, f_part)
    conv_grad = finish(lax.all_to_all(sums, ("yh", "yl"), 0, 0), taps, f_part, token)
    return (input_grad, conv_grad)


def solution(mesh):
    depth = mesh.shape["dp"] // Y_PARTS
    fine = Mesh(
        mesh.devices.reshape(depth // Z_PARTS, Z_PARTS, Y_PARTS, X_PARTS, Y_PARTS, CORES),
        ("zh", "zl", "yl", "x", "yh", "core"),
    )
    dp, seq = ("zh", "zl", "yl"), ("x", "yh", "core")
    return jax.shard_map(
        body,
        mesh=fine,
        in_specs=(P(dp, seq, None), P(None, dp, seq), P(seq, dp), P(dp, seq, None)),
        out_specs=(P(dp, seq, None), P(None, dp, seq)),
        check_vma=False,
    )
```
